768 devices in a mesh: shot: 128 (over x, y, z_hi, core), slab: 6 (over z_lo).
Axes of the slice: x: 4, y: 8, z: 12 (z_hi: 2, z_lo: 6; z = z_hi * 6 + z_lo), core: 2. Of those that a mesh axis runs over, the one named last changes fastest.
Arguments:
- velocity: float32 [128, 32, 96, 128], P('shot', None, 'slab'), may hold values from 0.15 to 0.45
- fwd_field: float32 [128, 64, 96, 256], P('shot', None, 'slab'), may hold values from -4 to 4
- adj_field: float32 [128, 64, 96, 256], P('shot', None, 'slab'), may hold values from -4 to 4
- aperture_anchor: int32 [128, 2], P('shot'), may hold values from 0 to 30, as said below
- source_cell: int32 [128, 16], P('shot'), may hold values from 0 to 1572863
- wavelet: float32 [128, 2, 16], P('shot'), may hold values from -6 to 6
- shot_count: int32 [128], P('shot'), may hold values from 1 to 16
- receiver_cell: int32 [128, 1024], P('shot'), may hold values from 0 to 1572863
- residual: float32 [128, 2, 1024], P('shot'), may hold values from -6 to 6
Outputs:
- gradient: float32 [128, 32, 96, 128], P('shot', None, 'slab')
The draws below stay inside these ranges and needn't reach their ends.
Inputs may be any that keep to these rules, and one draw needn't show every extreme that they name: `aperture_anchor`: entry g, 0 is g // 4 or one less and entry g, 1 is g % 4 or one less, each clipped so that the 2 x 2 tiles of the aperture lie in the model.
All inputs are finite; a program needn't handle non-finite values.
Results may differ from the reference program's by a relative error of at most 0.0003.
Values sent between devices are 32-bit elements; how exact they have to be, the bound alone decides.
No kernel may reach another device: no remote copies, remote signals or barrier semaphores. Data moves between devices by JAX's collectives and lax.ppermute only.
A program may use at most 64 MiB of HBM per device.

```python
import jax
import jax.numpy as jnp
from jax import lax

XT = 32
YT = 128
TILES_Y = 4
SHOTS = 16
RECV = 1024
STEPS = 2
GROUPS = 128
TILES = 128
AX = 64
AY = 256
NZ = 96


def draw_aperture_anchor(key, part):
    first_key, second_key = jax.random.split(jax.random.fold_in(key, 17))
    groups = jnp.arange(GROUPS, dtype=jnp.int32)
    tiles_x = GROUPS // TILES_Y
    step_row = jax.random.randint(first_key, (GROUPS,), -1, 1)
    step_col = jax.random.randint(second_key, (GROUPS,), -1, 1)
    anchor_row = jnp.clip(groups // TILES_Y + step_row, 0, tiles_x - 2)
    anchor_col = jnp.clip(groups % TILES_Y + step_col, 0, TILES_Y - 2)
    return jnp.stack([anchor_row, anchor_col], axis=1).astype(jnp.int32)


def touch_ends(result, own_key, smallest, high):
    place = [jax.random.randint(jax.random.fold_in(own_key, axis), (), 0, length) for axis, length in enumerate(result.shape)]
    widest = result.shape.index(max(result.shape))
    next_to = place[:widest] + [(place[widest] + 1) % result.shape[widest]] + place[widest + 1:]
    return result.at[tuple(place)].set(smallest).at[tuple(next_to)].set(high)


def shard_levels(key, dims, shards, smallest, largest):
    def one(axis_at, parts):
        steps = jax.random.uniform(jax.random.fold_in(jax.random.fold_in(key, 6), axis_at), (parts,), jnp.float32, smallest / len(shards), largest / len(shards))
        return jnp.repeat(jnp.exp(steps), dims[axis_at] // parts).reshape((-1,) + (1,) * (len(dims) - axis_at - 1))

    loudness = one(*shards[0])
    for cut in shards[1:]:
        loudness = loudness * one(*cut)
    return loudness


def normal_values(own_key, shape, spread, reach, cuts=(), held_as=jnp.bfloat16):
    loudness = shard_levels(own_key, shape, cuts, -0.22, 0.18) if cuts else 1.0
    result = jax.random.normal(own_key, shape, jnp.float32) * spread * loudness
    return jnp.minimum(jnp.maximum(result, -reach), reach).astype(held_as)


def setup_inputs(seed: int = 0) -> dict:
    arg_keys = jax.random.split(jax.random.key(seed), 10)
    velocity = jnp.clip(0.15 + 0.29999998 * jax.random.uniform(arg_keys[0], (TILES, XT, NZ, YT), jnp.float32) ** shard_levels(arg_keys[0], (TILES, XT, NZ, YT), ((0, 128), (2, 6)), -0.2, 0.2), 0.15, 0.45)
    fwd_field = normal_values(arg_keys[1], (GROUPS, AX, NZ, AY), 0.5, 4.0, ((0, 128), (2, 6)), jnp.float32)
    adj_field = normal_values(arg_keys[2], (GROUPS, AX, NZ, AY), 0.5, 4.0, ((0, 128), (2, 6)), jnp.float32)
    aperture_anchor = draw_aperture_anchor(jax.random.fold_in(arg_keys[9], 71), 0)
    source_cell = touch_ends(jax.random.randint(arg_keys[4], (GROUPS, SHOTS), 0, AX * NZ * AY), jax.random.fold_in(arg_keys[4], 1), 0, (AX * NZ * AY) - 1).astype(jnp.int32)
    wavelet = normal_values(arg_keys[5], (GROUPS, STEPS, SHOTS), 1.0, 6.0, ((0, 128),), jnp.float32)
    shot_count = touch_ends(jax.random.randint(arg_keys[6], (GROUPS,), 1, SHOTS + 1), jax.random.fold_in(arg_keys[6], 1), 1, SHOTS).astype(jnp.int32)
    receiver_cell = touch_ends(jax.random.randint(arg_keys[7], (GROUPS, RECV), 0, AX * NZ * AY), jax.random.fold_in(arg_keys[7], 1), 0, (AX * NZ * AY) - 1).astype(jnp.int32)
    residual = normal_values(arg_keys[8], (GROUPS, STEPS, RECV), 1.0, 6.0, ((0, 128),), jnp.float32)
    return dict(velocity=velocity, fwd_field=fwd_field, adj_field=adj_field, aperture_anchor=aperture_anchor, source_cell=source_cell, wavelet=wavelet, shot_count=shot_count, receiver_cell=receiver_cell, residual=residual)


CENTRE = -205.0 / 72.0
STENCIL = (1.6, -0.2, 8.0 / 315.0, -1.0 / 560.0)


def laplace(padded_z):
    inner_depth = padded_z.shape[1] - 8
    padded = jnp.pad(padded_z, ((4, 4), (0, 0), (4, 4)))
    along_x = padded_z.shape[0]
    along_y = padded_z.shape[2]

    def window(shift_x, shift_z, shift_y):
        return padded[4 + shift_x:4 + shift_x + along_x, 4 + shift_z:4 + shift_z + inner_depth, 4 + shift_y:4 + shift_y + along_y]

    summed = (3.0 * CENTRE) * window(0, 0, 0)
    for distance in range(1, 5):
        paired = window(distance, 0, 0) + window(-distance, 0, 0)
        paired = paired + window(0, distance, 0) + window(0, -distance, 0)
        paired = paired + window(0, 0, distance) + window(0, 0, -distance)
        summed = summed + STENCIL[distance - 1] * paired
    return summed


def inject(field, positions, amounts):
    return field.reshape(-1).at[positions].add(amounts).reshape(field.shape)


def advance(initial, coefficient, positions, first_amounts, second_amounts):
    first_change = inject(coefficient * laplace(jnp.pad(initial, ((0, 0), (4, 4), (0, 0)))), positions, first_amounts)
    middle = initial + first_change
    second_change = inject(coefficient * laplace(jnp.pad(middle, ((0, 0), (4, 4), (0, 0)))), positions, second_amounts)
    return first_change, second_change


def reference(velocity, fwd_field, adj_field, aperture_anchor, source_cell, wavelet, shot_count, receiver_cell, residual):
    row_step = jnp.array([0, 0, 1, 1], dtype=jnp.int32)
    col_step = jnp.array([0, 1, 0, 1], dtype=jnp.int32)

    def one_group(summed, group_index):
        anchor_row = aperture_anchor[group_index, 0]
        anchor_col = aperture_anchor[group_index, 1]
        tile_ids = ((anchor_row + row_step) * TILES_Y + anchor_col + col_step).astype(jnp.int32)
        tiles = velocity[tile_ids].reshape(2, 2, XT, NZ, YT)
        speeds = tiles.transpose(0, 2, 3, 1, 4).reshape(2 * XT, NZ, 2 * YT)
        coefficient = speeds * speeds
        active = (jnp.arange(SHOTS, dtype=jnp.int32) < shot_count[group_index]).astype(jnp.float32)
        first_change, second_change = advance(fwd_field[group_index], coefficient, source_cell[group_index],
                                              wavelet[group_index, 0] * active, wavelet[group_index, 1] * active)
        start_adjoint = adj_field[group_index]
        back_first, back_second = advance(start_adjoint, coefficient, receiver_cell[group_index],
                                          residual[group_index, 1], residual[group_index, 0])
        later = start_adjoint + back_first
        earlier = 2.0 * later - start_adjoint + back_second
        imaged = earlier * first_change + later * second_change
        pieces = imaged.reshape(2, XT, NZ, 2, YT).transpose(0, 3, 1, 2, 4).reshape(4, XT, NZ, YT)
        return summed.at[tile_ids].add(pieces), None

    summed, unused = lax.scan(one_group, jnp.zeros(velocity.shape, jnp.float32), jnp.arange(GROUPS, dtype=jnp.int32))
    return 2.0 * velocity * summed
```

```python
import jax
import jax.numpy as jnp
import numpy as np
from jax import lax
from jax.experimental import pallas as pl
from jax.experimental.pallas import tpu as pltpu
from jax.sharding import PartitionSpec as P

TILES_Y = 4
CENTRE = -205.0 / 72.0
STENCIL = (1.6, -0.2, 8.0 / 315.0, -1.0 / 560.0)

BX = 8
Z = 16
Y = 256
AX = 64
ROWS = BX * Z
BLOCKS = AX // BX
FLAT = AX * Z
F32 = jnp.float32
BF16 = jnp.bfloat16
VMEM = pl.BlockSpec(memory_space=pltpu.VMEM)
SMEM = pl.BlockSpec(memory_space=pltpu.SMEM)


def weight(distance):
    distance = np.abs(distance)
    table = np.array((0.0,) + STENCIL + (0.0,))
    return table[np.minimum(distance, 5)]


def parts_of(matrix):
    high = matrix.astype(np.float32).astype(jnp.bfloat16)
    low = (matrix - high.astype(np.float64)).astype(np.float32).astype(jnp.bfloat16)
    return high, low


def along_xz():
    out_x, out_z = np.divmod(np.arange(ROWS), Z)
    in_x, in_z = np.divmod(np.arange(2 * ROWS), Z)
    kinds = []
    for lead in (0, 4, 8):
        dx = out_x[:, None] - (in_x[None, :] - lead)
        dz = out_z[:, None] - in_z[None, :]
        both = np.where(dz == 0, weight(dx), 0.0) + np.where(dx == 0, weight(dz), 0.0)
        kinds.append(both + np.where((dx == 0) & (dz == 0), 3.0 * CENTRE, 0.0))
    return np.stack(kinds)


def along_y():
    at = np.arange(Y)
    return weight(at[:, None] - at[None, :])


def along_halo():
    out_x, out_z = np.divmod(np.arange(ROWS), Z)
    in_x, in_s = np.divmod(np.arange(BX * 8), 8)
    fields = []
    for field in (0, 1):
        sides = []
        for side in (0, 1):
            layer = in_s - 4 * field
            depth = layer - 4 if side == 0 else Z + layer
            mine = (layer >= 0) & (layer < 4)
            dz = out_z[:, None] - depth[None, :]
            same = (out_x[:, None] == in_x[None, :]) & mine[None, :]
            sides.append(np.where(same, weight(dz), 0.0))
        fields.append(np.concatenate(sides, 1))
    return np.concatenate(fields, 0)


def dot(a, b):
    return jnp.dot(a, b, preferred_element_type=F32)


def split(value):
    high = value.astype(BF16)
    return high, (value - high.astype(F32)).astype(BF16)


def cost(flops, nbytes):
    return pl.CostEstimate(flops=flops, transcendentals=0, bytes_accessed=nbytes)


def params():
    return pltpu.CompilerParams(vmem_limit_bytes=40 * 1024 * 1024)


def rims(fwd, adj):
    front = lax.broadcasted_iota(jnp.int32, (BX, 8, Y), 1) < 4
    top = jnp.where(front, pltpu.roll(fwd[:, 8:, :], 4, 1), adj[:, 8:, :])
    bottom = jnp.where(front, fwd[:, :8, :], pltpu.roll(adj[:, :8, :], 4, 1))
    return top, bottom


def pack_kernel(sides, vel, fwd, adj, up, down, tagged):
    def step(b, _):
        at = pl.ds(b * BX, BX)
        up[at], down[at] = rims(fwd[at], adj[at])
        return 0

    lax.fori_loop(0, BLOCKS, step, 0)
    rows = vel.shape[0]
    tagged[:rows] = vel[...]
    half = lax.broadcasted_iota(jnp.int32, tagged.shape[1:], 0) < 8
    tagged[rows] = jnp.where(half, sides[0].astype(F32), sides[1].astype(F32))


def inner_laplace(b, high, low, s_high, s_low, y_high, y_low):
    kind = jnp.where(b == 0, 0, jnp.where(b == BLOCKS - 1, 2, 1))
    first = jnp.clip(b * BX - 4, 0, AX - 2 * BX) * Z
    window = pl.ds(pl.multiple_of(first, 64), 2 * ROWS)
    own = pl.ds(pl.multiple_of(b * ROWS, ROWS), ROWS)
    wide = high[window]
    near = high[own]
    result = dot(s_high[kind], wide) + dot(near, y_high[...])
    result = result + dot(s_high[kind], low[window]) + dot(low[own], y_high[...])
    return result + dot(s_low[kind], wide) + dot(near, y_low[...])


def split_all(field, high, low):
    def step(b, _):
        at = pl.ds(pl.multiple_of(b * ROWS, ROWS), ROWS)
        high[at], low[at] = split(field[at])
        return 0

    lax.fori_loop(0, BLOCKS, step, 0)


def columns_of(points, columns):
    turned = points[...].T
    count = turned.shape[0]

    def step(i, _):
        at = pl.ds(pl.multiple_of(i * 128, 128), 128)
        part = points[:, at].T
        here = lax.broadcasted_iota(jnp.int32, (128, Y), 1) == part[:, 1:2].astype(jnp.int32)
        for n in range(2):
            high, low = split(part[:, 2 + n : 3 + n])
            columns[at, pl.ds(2 * n * Y, Y)] = jnp.where(here, high.astype(F32), 0.0).astype(BF16)
            columns[at, pl.ds((2 * n + 1) * Y, Y)] = jnp.where(here, low.astype(F32), 0.0).astype(BF16)
        return 0

    lax.fori_loop(0, count // 128, step, 0)


def injected(b, points, columns):
    rows = lax.broadcasted_iota(jnp.int32, (ROWS, points.shape[1]), 0) + b * ROWS
    hot = jnp.where(rows == points[0:1, :].astype(jnp.int32), 1.0, 0.0).astype(BF16)
    first = dot(hot, columns[:, : 2 * Y])
    second = dot(hot, columns[:, 2 * Y :])
    return first[:, :Y] + first[:, Y:], second[:, :Y] + second[:, Y:]


def first_kernel(fwd, adj, shots, receivers, s_high, s_low, y_high, y_low,
                 lap_fwd, lap_adj, fwd_in1, fwd_in2, adj_in1, adj_in2,
                 fh, fl, ah, al, shot_columns, receiver_columns):
    split_all(fwd, fh, fl)
    split_all(adj, ah, al)
    columns_of(shots, shot_columns)
    columns_of(receivers, receiver_columns)

    def step(b, _):
        at = pl.ds(pl.multiple_of(b * ROWS, ROWS), ROWS)
        lap_fwd[at] = inner_laplace(b, fh, fl, s_high, s_low, y_high, y_low)
        lap_adj[at] = inner_laplace(b, ah, al, s_high, s_low, y_high, y_low)
        fwd_in1[at], fwd_in2[at] = injected(b, shots, shot_columns)
        adj_in1[at], adj_in2[at] = injected(b, receivers, receiver_columns)
        return 0

    lax.fori_loop(0, BLOCKS, step, 0)


def laplace_kernel(fwd, adj, s_high, s_low, y_high, y_low, lap_fwd, lap_adj, fh, fl, ah, al):
    split_all(fwd, fh, fl)
    split_all(adj, ah, al)

    def step(b, _):
        at = pl.ds(pl.multiple_of(b * ROWS, ROWS), ROWS)
        lap_fwd[at] = inner_laplace(b, fh, fl, s_high, s_low, y_high, y_low)
        lap_adj[at] = inner_laplace(b, ah, al, s_high, s_low, y_high, y_low)
        return 0

    lax.fori_loop(0, BLOCKS, step, 0)


def halo_part(b, below, above, h_high, h_low):
    at = pl.ds(pl.multiple_of(b * (ROWS // 2), ROWS // 2), ROWS // 2)
    high, low = split(jnp.concatenate([below[at], above[at]], 0))
    both = dot(h_high[...], high) + dot(h_high[...], low) + dot(h_low[...], high)
    return both[:ROWS], both[ROWS:]


def advance_kernel(flags, own, col_a, col_b, row_e, row_o, diag_e, diag_o, lap_fwd, lap_adj, fwd, adj, fwd_in, adj_in,
                   below, above, h_high, h_low, speed2, mid_fwd, mid_adj, up, down):
    half = own.shape[0]
    wide = own.shape[2]
    with_e = flags[2] == 1
    with_a = flags[3] == 1
    row_at = flags[0] * half
    row_to = (1 - flags[0]) * half
    col_at = pl.ds(pl.multiple_of(flags[1] * wide, wide), wide)
    col_to = pl.ds(pl.multiple_of((1 - flags[1]) * wide, wide), wide)

    def assemble(i, _):
        at = pl.ds(i * 8, 8)
        near = pl.ds(row_at + i * 8, 8)
        far = pl.ds(row_to + i * 8, 8)
        speed = own[at]
        speed2[near, :, col_at] = speed * speed
        speed = jnp.where(with_a, col_a[at], col_b[at])
        speed2[near, :, col_to] = speed * speed
        speed = jnp.where(with_e, row_e[at], row_o[at])
        speed2[far, :, col_at] = speed * speed
        speed = jnp.where(with_e, diag_e[at], diag_o[at])
        speed2[far, :, col_to] = speed * speed
        return 0

    lax.fori_loop(0, half // 8, assemble, 0)

    def step(b, _):
        at = pl.ds(pl.multiple_of(b * ROWS, ROWS), ROWS)
        blk = pl.ds(b * BX, BX)
        halo_fwd, halo_adj = halo_part(b, below, above, h_high, h_low)
        c = speed2[blk].reshape(ROWS, Y)
        new_fwd = fwd[at] + (c * (lap_fwd[at] + halo_fwd) + fwd_in[at])
        new_adj = adj[at] + (c * (lap_adj[at] + halo_adj) + adj_in[at])
        mid_fwd[at] = new_fwd
        mid_adj[at] = new_adj
        up[blk], down[blk] = rims(new_fwd.reshape(BX, Z, Y), new_adj.reshape(BX, Z, Y))
        return 0

    lax.fori_loop(0, BLOCKS, step, 0)


def image_kernel(flags, speed2, lap_fwd, lap_adj, fwd, adj, mid_fwd, mid_adj, fwd_in, adj_in, below, above, h_high, h_low,
                 own, col, row, diag, image):
    def step(b, _):
        at = pl.ds(pl.multiple_of(b * ROWS, ROWS), ROWS)
        halo_fwd, halo_adj = halo_part(b, below, above, h_high, h_low)
        c = speed2[at]
        second_fwd = c * (lap_fwd[at] + halo_fwd) + fwd_in[at]
        second_adj = c * (lap_adj[at] + halo_adj) + adj_in[at]
        later = mid_adj[at]
        earlier = 2.0 * later - adj[at] + second_adj
        imaged = earlier * (mid_fwd[at] - fwd[at]) + later * second_fwd
        image[pl.ds(b * BX, BX)] = imaged.reshape(BX, Z, Y)
        return 0

    lax.fori_loop(0, BLOCKS, step, 0)
    half = own.shape[0]
    wide = own.shape[2]
    row_at = flags[0] * half
    row_to = (1 - flags[0]) * half
    col_at = pl.ds(pl.multiple_of(flags[1] * wide, wide), wide)
    col_to = pl.ds(pl.multiple_of((1 - flags[1]) * wide, wide), wide)

    def hand_out(i, _):
        at = pl.ds(i * 8, 8)
        near = pl.ds(row_at + i * 8, 8)
        far = pl.ds(row_to + i * 8, 8)
        own[at] = image[near, :, col_at]
        col[at] = image[near, :, col_to]
        row[at] = image[far, :, col_at]
        diag[at] = image[far, :, col_to]
        return 0

    lax.fori_loop(0, half // 8, hand_out, 0)


def swaps(count):
    rows = count // TILES_Y
    a = [(s, s ^ 1) for s in range(count)]
    b = [(s, s + 1) if s % TILES_Y == 1 else (s, s - 1) for s in range(count) if s % TILES_Y in (1, 2)]
    e = [(s, s + TILES_Y if (s // TILES_Y) % 2 == 0 else s - TILES_Y) for s in range(count)]
    o = []
    for s in range(count):
        other = s // TILES_Y + (1 if (s // TILES_Y) % 2 else -1)
        if 0 <= other < rows:
            o.append((s, other * TILES_Y + s % TILES_Y))
    return a, b, e, o


def point_table(cells, amounts, first_layer, total_depth, plane, width):
    cell_x = cells // (total_depth * plane)
    cell_z = cells // plane % total_depth - first_layer
    inside = (cell_z >= 0) & (cell_z < Z)
    row = jnp.where(inside, cell_x * Z + cell_z, -1)
    table = jnp.stack([row.astype(F32), (cells % plane).astype(F32), amounts[0], amounts[1]])
    table = jnp.pad(table, ((0, 4), (0, 0)))
    if cells.shape[0] < width:
        table = jnp.pad(table, ((0, 0), (0, width - cells.shape[0])), constant_values=-1.0)
    return table


def body(velocity, fwd_field, adj_field, aperture_anchor, source_cell, wavelet, shot_count, receiver_cell, residual):
    tile = velocity[0]
    half, depth, wide = tile.shape
    slabs = lax.axis_size("slab")
    total_depth = depth * slabs
    first_layer = lax.axis_index("slab") * depth
    device = lax.axis_index("shot")
    home_row = device // TILES_Y
    home_col = device % TILES_Y
    pair_a, pair_b, pair_e, pair_o = swaps(lax.axis_size("shot"))
    to_up = [(i, i + 1) for i in range(slabs - 1)]
    to_down = [(i + 1, i) for i in range(slabs - 1)]
    part_row = home_row - aperture_anchor[0, 0]
    part_col = home_col - aperture_anchor[0, 1]
    side_row = 1 - 2 * part_row
    side_col = 1 - 2 * part_col
    toward_e = 1 - 2 * (home_row % 2)
    toward_a = 1 - 2 * (home_col % 2)
    with_e = side_row == toward_e
    with_a = side_col == toward_a
    flags = jnp.stack([part_row, part_col, with_e.astype(jnp.int32), with_a.astype(jnp.int32)])

    def shape(*dims, dtype=F32):
        return jax.ShapeDtypeStruct(dims, dtype)

    def along(pairs, value):
        return lax.ppermute(value, "shot", pairs)

    col_b = along(pair_b, tile)
    col_a = along(pair_a, tile)
    fwd = fwd_field[0]
    adj = adj_field[0]
    up, down, tagged = pl.pallas_call(
        pack_kernel,
        name="pack",
        out_shape=(shape(AX, 8, Y), shape(AX, 8, Y), shape(half + 1, depth, wide)),
        in_specs=[SMEM, VMEM, VMEM, VMEM],
        out_specs=(VMEM, VMEM, VMEM),
        compiler_params=params(),
        cost_estimate=cost(1 << 20, 5 << 20),
    )(jnp.stack([side_row, side_col]), tile, fwd, adj)
    row_e = along(pair_e, tagged)
    row_o = along(pair_o, tagged)
    below = lax.ppermute(up, "slab", to_up)
    above = lax.ppermute(down, "slab", to_down)

    s_high, s_low = parts_of(along_xz())
    y_high, y_low = parts_of(along_y())
    h_high, h_low = parts_of(along_halo())
    inner = tuple(jnp.asarray(m) for m in (s_high, s_low, y_high, y_low))
    rim = tuple(jnp.asarray(m) for m in (h_high, h_low))

    active = (jnp.arange(source_cell.shape[1], dtype=jnp.int32) < shot_count[0]).astype(F32)
    shots = point_table(source_cell[0], wavelet[0] * active, first_layer, total_depth, Y, 128)
    receivers = point_table(receiver_cell[0], residual[0, ::-1], first_layer, total_depth, Y, receiver_cell.shape[1])
    flat_fwd = fwd.reshape(FLAT, Y)
    flat_adj = adj.reshape(FLAT, Y)
    flat = shape(FLAT, Y)
    halves = [pltpu.VMEM((FLAT, Y), BF16)] * 4
    lap_fwd, lap_adj, fwd_in1, fwd_in2, adj_in1, adj_in2 = pl.pallas_call(
        first_kernel,
        name="first",
        out_shape=(flat,) * 6,
        in_specs=[VMEM] * 8,
        out_specs=(VMEM,) * 6,
        scratch_shapes=halves + [pltpu.VMEM((shots.shape[1], 4 * Y), BF16), pltpu.VMEM((receivers.shape[1], 4 * Y), BF16)],
        compiler_params=params(),
        cost_estimate=cost(5 << 30, 9 << 20),
    )(flat_fwd, flat_adj, shots, receivers, *inner)

    e_row = row_e[half, 0, 0]
    e_col = row_e[half, depth - 1, 0]
    o_row = row_o[half, 0, 0]
    o_col = row_o[half, depth - 1, 0]
    a_side = toward_a.astype(F32)
    diag_e = along(pair_e, jnp.where(e_col == a_side, col_a, col_b))
    diag_o = along(pair_o, jnp.where(o_col == a_side, col_a, col_b))

    speed2, mid_fwd, mid_adj, up, down = pl.pallas_call(
        advance_kernel,
        name="advance",
        out_shape=(shape(AX, depth, Y), flat, flat, shape(AX, 8, Y), shape(AX, 8, Y)),
        in_specs=[SMEM] + [VMEM] * 17,
        out_specs=(VMEM,) * 5,
        compiler_params=params(),
        cost_estimate=cost(1 << 30, 12 << 20),
    )(flags, tile, col_a, col_b, row_e, row_o, diag_e, diag_o, lap_fwd, lap_adj, flat_fwd, flat_adj, fwd_in1, adj_in1,
      below.reshape(AX * 8, Y), above.reshape(AX * 8, Y), *rim)
    below = lax.ppermute(up, "slab", to_up)
    above = lax.ppermute(down, "slab", to_down)
    lap_fwd, lap_adj = pl.pallas_call(
        laplace_kernel,
        name="second",
        out_shape=(flat,) * 2,
        in_specs=[VMEM] * 6,
        out_specs=(VMEM,) * 2,
        scratch_shapes=halves,
        compiler_params=params(),
        cost_estimate=cost(2 << 30, 5 << 20),
    )(mid_fwd, mid_adj, *inner)
    piece = shape(half, depth, wide)
    own, col, row, diag = pl.pallas_call(
        image_kernel,
        name="image",
        out_shape=(piece,) * 4,
        in_specs=[SMEM] + [VMEM] * 13,
        out_specs=(VMEM,) * 4,
        scratch_shapes=[pltpu.VMEM((AX, depth, Y), F32)],
        compiler_params=params(),
        cost_estimate=cost(1 << 30, 11 << 20),
    )(flags, speed2.reshape(FLAT, Y), lap_fwd, lap_adj, flat_fwd, flat_adj, mid_fwd, mid_adj, fwd_in2, adj_in2,
      below.reshape(AX * 8, Y), above.reshape(AX * 8, Y), *rim)

    from_e = e_row == -toward_e.astype(F32)
    from_o = o_row == toward_e.astype(F32)
    back_e = along(pair_e, diag)
    back_o = along(pair_o, diag)
    same_e = along(pair_e, row)
    same_o = along(pair_o, row)

    def bucket(mine, side):
        total = jnp.where(mine, col, 0.0)
        total = total + jnp.where(from_e & (e_col == side), back_e, 0.0)
        return total + jnp.where(from_o & (o_col == side), back_o, 0.0)

    sum_b = along(pair_b, bucket(~with_a, -a_side))
    sum_a = along(pair_a, bucket(with_a, a_side))
    summed = own + jnp.where(from_e, same_e, 0.0) + jnp.where(from_o, same_o, 0.0) + sum_a + sum_b
    return (2.0 * tile * summed)[None]


def solution(mesh):
    placed = (
        P("shot", None, "slab", None),
        P("shot", None, "slab", None),
        P("shot", None, "slab", None),
        P("shot", None),
        P("shot", None),
        P("shot", None, None),
        P("shot"),
        P("shot", None),
        P("shot", None, None),
    )
    return jax.shard_map(body, mesh=mesh, in_specs=placed, out_specs=P("shot", None, "slab", None), check_vma=False)
```

```python
import functools

import jax
import jax.numpy as jnp
import numpy as np
from jax import lax
from jax.experimental import pallas as pl
from jax.experimental.pallas import tpu as pltpu
from jax.sharding import PartitionSpec as P


TILES_Y = 4
CENTRE = -205.0 / 72.0
STENCIL = (1.6, -0.2, 8.0 / 315.0, -1.0 / 560.0)

BX = 8
Z = 16
Y = 256
Y_BITS = 8
AX = 64
ROWS = BX * Z
BLOCKS = AX // BX
FLAT = AX * Z
F32 = jnp.float32
BF16 = jnp.bfloat16
VMEM = pl.BlockSpec(memory_space=pltpu.VMEM)
SMEM = pl.BlockSpec(memory_space=pltpu.SMEM)


def weight(distance):
    distance = np.abs(distance)
    table = np.array((0.0,) + STENCIL + (0.0,))
    return table[np.minimum(distance, 5)]


def parts_of(matrix):
    high = matrix.astype(np.float32).astype(jnp.bfloat16)
    low = (matrix - high.astype(np.float64)).astype(np.float32).astype(jnp.bfloat16)
    return high, low


def along_xz():
    out_x, out_z = np.divmod(np.arange(ROWS), Z)
    in_x, in_z = np.divmod(np.arange(2 * ROWS), Z)
    kinds = []
    for lead in (0, 4, 8):
        dx = out_x[:, None] - (in_x[None, :] - lead)
        dz = out_z[:, None] - in_z[None, :]
        both = np.where(dz == 0, weight(dx), 0.0) + np.where(dx == 0, weight(dz), 0.0)
        kinds.append(both + np.where((dx == 0) & (dz == 0), 3.0 * CENTRE, 0.0))
    return np.stack(kinds)


def along_y():
    at = np.arange(Y)
    return weight(at[:, None] - at[None, :])


def along_halo():
    out_x, out_z = np.divmod(np.arange(ROWS), Z)
    in_x, in_s = np.divmod(np.arange(BX * 8), 8)
    fields = []
    for field in (0, 1):
        sides = []
        for side in (0, 1):
            layer = in_s - 4 * field
            depth = layer - 4 if side == 0 else Z + layer
            mine = (layer >= 0) & (layer < 4)
            dz = out_z[:, None] - depth[None, :]
            same = (out_x[:, None] == in_x[None, :]) & mine[None, :]
            sides.append(np.where(same, weight(dz), 0.0))
        fields.append(np.concatenate(sides, 1))
    return np.concatenate(fields, 0)


def dot(a, b):
    return jnp.dot(a, b, preferred_element_type=F32)


def split(value):
    high = value.astype(BF16)
    return high, (value - high.astype(F32)).astype(BF16)


def cost(flops, nbytes):
    return pl.CostEstimate(flops=flops, transcendentals=0, bytes_accessed=nbytes)


def rims(fwd, adj):
    front = lax.broadcasted_iota(jnp.int32, (BX, 8, Y), 1) < 4
    top = jnp.where(front, pltpu.roll(fwd[:, 8:, :], 4, 1), adj[:, 8:, :])
    bottom = jnp.where(front, fwd[:, :8, :], pltpu.roll(adj[:, :8, :], 4, 1))
    return top, bottom


def pack_kernel(anchor, vel, fwd, adj, up, down, tagged, flags):
    device = lax.axis_index("shot")
    home_row = device // TILES_Y
    home_col = device - home_row * TILES_Y
    part_row = home_row - anchor[0, 0]
    part_col = home_col - anchor[0, 1]
    side_row = 1 - 2 * part_row
    side_col = 1 - 2 * part_col
    toward_e = 1 - 2 * (home_row & 1)
    toward_a = 1 - 2 * (home_col & 1)
    flags[0] = part_row
    flags[1] = part_col
    flags[2] = jnp.where(side_row == toward_e, 1, 0)
    flags[3] = jnp.where(side_col == toward_a, 1, 0)
    flags[4] = toward_e
    flags[5] = toward_a
    rows = vel.shape[0]
    tagged[rows] = jnp.full(tagged.shape[1:], side_row.astype(F32))
    tagged[rows + 1] = jnp.full(tagged.shape[1:], side_col.astype(F32))

    def step(b, _):
        at = pl.ds(b * BX, BX)
        up[at], down[at] = rims(fwd[at], adj[at])
        return 0

    lax.fori_loop(0, BLOCKS, step, 0)

    def copy(i, _):
        at = pl.ds(i * 8, 8)
        tagged[at] = vel[at]
        return 0

    lax.fori_loop(0, rows // 8, copy, 0)


def inner_laplace(b, high, low, s_high, s_low, y_high, y_low):
    kind = jnp.where(b == 0, 0, jnp.where(b == BLOCKS - 1, 2, 1))
    first = jnp.clip(b * BX - 4, 0, AX - 2 * BX) * Z
    window = pl.ds(pl.multiple_of(first, 64), 2 * ROWS)
    own = pl.ds(pl.multiple_of(b * ROWS, ROWS), ROWS)
    wide = high[window]
    near = high[own]
    result = dot(s_high[kind], wide) + dot(near, y_high[...])
    result = result + dot(s_high[kind], low[window]) + dot(low[own], y_high[...])
    return result + dot(s_low[kind], wide) + dot(near, y_low[...])


def split_all(field, high, low):
    def step(b, _):
        at = pl.ds(pl.multiple_of(b * ROWS, ROWS), ROWS)
        high[at], low[at] = split(field[at])
        return 0

    lax.fori_loop(0, BLOCKS, step, 0)


def table_of(cells, amounts, first_layer, total_depth, table):
    count = cells.shape[1]
    column = cells >> Y_BITS
    cell_x = ((column.astype(F32) + 0.5) * (1.0 / total_depth)).astype(jnp.int32)
    cell_z = column - cell_x * total_depth - first_layer
    inside = (cell_z >= 0) & (cell_z < Z)
    table[...] = jnp.full(table.shape, -1.0, F32)
    table[0:1, 0:count] = jnp.where(inside, cell_x * Z + cell_z, -1).astype(F32)
    table[1:2, 0:count] = (cells & (Y - 1)).astype(F32)
    table[2:3, 0:count] = amounts[0]
    table[3:4, 0:count] = amounts[1]


def columns_of(points, columns):
    def step(i, _):
        at = pl.ds(pl.multiple_of(i * 128, 128), 128)
        part = points[:, at].T
        here = lax.broadcasted_iota(jnp.int32, (128, Y), 1) == part[:, 1:2].astype(jnp.int32)
        for n in range(2):
            high, low = split(part[:, 2 + n : 3 + n])
            columns[at, pl.ds(2 * n * Y, Y)] = jnp.where(here, high.astype(F32), 0.0).astype(BF16)
            columns[at, pl.ds((2 * n + 1) * Y, Y)] = jnp.where(here, low.astype(F32), 0.0).astype(BF16)
        return 0

    lax.fori_loop(0, points.shape[1] // 128, step, 0)


def injected(b, points, columns):
    rows = lax.broadcasted_iota(jnp.int32, (ROWS, points.shape[1]), 0) + b * ROWS
    hot = jnp.where(rows == points[0:1, :].astype(jnp.int32), 1.0, 0.0).astype(BF16)
    first = dot(hot, columns[:, : 2 * Y])
    second = dot(hot, columns[:, 2 * Y :])
    return first[:, :Y] + first[:, Y:], second[:, :Y] + second[:, Y:]


def inject_kernel(total_depth, shot_count, source_cell, wavelet, receiver_cell, residual, fwd_in1, fwd_in2, adj_in1, adj_in2,
                  shots, receivers, shot_columns, receiver_columns):
    first_layer = lax.axis_index("slab") * Z
    active = lax.broadcasted_iota(jnp.int32, source_cell.shape, 1) < shot_count[0]
    waves = [jnp.where(active, wavelet[n : n + 1, :], 0.0) for n in range(2)]
    table_of(source_cell[...], waves, first_layer, total_depth, shots)
    table_of(receiver_cell[...], [residual[1:2, :], residual[0:1, :]], first_layer, total_depth, receivers)
    columns_of(shots, shot_columns)
    columns_of(receivers, receiver_columns)

    def step(b, _):
        at = pl.ds(pl.multiple_of(b * ROWS, ROWS), ROWS)
        fwd_in1[at], fwd_in2[at] = injected(b, shots, shot_columns)
        adj_in1[at], adj_in2[at] = injected(b, receivers, receiver_columns)
        return 0

    lax.fori_loop(0, BLOCKS, step, 0)


def laplace_kernel(fwd, adj, s_high, s_low, y_high, y_low, lap_fwd, lap_adj, fh, fl, ah, al):
    split_all(fwd, fh, fl)
    split_all(adj, ah, al)

    def step(b, _):
        at = pl.ds(pl.multiple_of(b * ROWS, ROWS), ROWS)
        lap_fwd[at] = inner_laplace(b, fh, fl, s_high, s_low, y_high, y_low)
        lap_adj[at] = inner_laplace(b, ah, al, s_high, s_low, y_high, y_low)
        return 0

    lax.fori_loop(0, BLOCKS, step, 0)


def halo_part(b, below, above, h_high, h_low):
    at = pl.ds(pl.multiple_of(b * (ROWS // 2), ROWS // 2), ROWS // 2)
    high, low = split(jnp.concatenate([below[at], above[at]], 0))
    both = dot(h_high[...], high) + dot(h_high[...], low) + dot(h_low[...], high)
    return both[:ROWS], both[ROWS:]


def advance_kernel(flags, own, col_a, col_b, row_e, row_o, diag_e, diag_o, lap_fwd, lap_adj, fwd, adj, fwd_in, adj_in,
                   below, above, h_high, h_low, speed2, mid_fwd, mid_adj, up, down):
    half = own.shape[0]
    wide = own.shape[2]
    with_e = flags[2] == 1
    with_a = flags[3] == 1
    row_at = flags[0] * half
    row_to = (1 - flags[0]) * half
    col_at = pl.ds(pl.multiple_of(flags[1] * wide, wide), wide)
    col_to = pl.ds(pl.multiple_of((1 - flags[1]) * wide, wide), wide)

    def assemble(i, _):
        at = pl.ds(i * 8, 8)
        near = pl.ds(row_at + i * 8, 8)
        far = pl.ds(row_to + i * 8, 8)
        speed = own[at]
        speed2[near, :, col_at] = speed * speed
        speed = jnp.where(with_a, col_a[at], col_b[at])
        speed2[near, :, col_to] = speed * speed
        speed = jnp.where(with_e, row_e[at], row_o[at])
        speed2[far, :, col_at] = speed * speed
        speed = jnp.where(with_e, diag_e[at], diag_o[at])
        speed2[far, :, col_to] = speed * speed
        return 0

    lax.fori_loop(0, half // 8, assemble, 0)

    def step(b, _):
        at = pl.ds(pl.multiple_of(b * ROWS, ROWS), ROWS)
        blk = pl.ds(b * BX, BX)
        halo_fwd, halo_adj = halo_part(b, below, above, h_high, h_low)
        c = speed2[blk].reshape(ROWS, Y)
        new_fwd = fwd[at] + (c * (lap_fwd[at] + halo_fwd) + fwd_in[at])
        new_adj = adj[at] + (c * (lap_adj[at] + halo_adj) + adj_in[at])
        mid_fwd[at] = new_fwd
        mid_adj[at] = new_adj
        up[blk], down[blk] = rims(new_fwd.reshape(BX, Z, Y), new_adj.reshape(BX, Z, Y))
        return 0

    lax.fori_loop(0, BLOCKS, step, 0)


def image_kernel(flags, speed2, lap_fwd, lap_adj, fwd, adj, mid_fwd, mid_adj, fwd_in, adj_in, below, above, h_high, h_low,
                 own, col, row, diag, image):
    def step(b, _):
        at = pl.ds(pl.multiple_of(b * ROWS, ROWS), ROWS)
        halo_fwd, halo_adj = halo_part(b, below, above, h_high, h_low)
        c = speed2[at]
        second_fwd = c * (lap_fwd[at] + halo_fwd) + fwd_in[at]
        second_adj = c * (lap_adj[at] + halo_adj) + adj_in[at]
        later = mid_adj[at]
        earlier = 2.0 * later - adj[at] + second_adj
        imaged = earlier * (mid_fwd[at] - fwd[at]) + later * second_fwd
        image[pl.ds(b * BX, BX)] = imaged.reshape(BX, Z, Y)
        return 0

    lax.fori_loop(0, BLOCKS, step, 0)
    half = own.shape[0]
    wide = own.shape[2]
    row_at = flags[0] * half
    row_to = (1 - flags[0]) * half
    col_at = pl.ds(pl.multiple_of(flags[1] * wide, wide), wide)
    col_to = pl.ds(pl.multiple_of((1 - flags[1]) * wide, wide), wide)

    def hand_out(i, _):
        at = pl.ds(i * 8, 8)
        near = pl.ds(row_at + i * 8, 8)
        far = pl.ds(row_to + i * 8, 8)
        own[at] = image[near, :, col_at]
        col[at] = image[near, :, col_to]
        row[at] = image[far, :, col_at]
        diag[at] = image[far, :, col_to]
        return 0

    lax.fori_loop(0, half // 8, hand_out, 0)


def swaps(count):
    rows = count // TILES_Y
    a = [(s, s ^ 1) for s in range(count)]
    b = [(s, s + 1) if s % TILES_Y == 1 else (s, s - 1) for s in range(count) if s % TILES_Y in (1, 2)]
    e = [(s, s + TILES_Y if (s // TILES_Y) % 2 == 0 else s - TILES_Y) for s in range(count)]
    o = []
    for s in range(count):
        other = s // TILES_Y + (1 if (s // TILES_Y) % 2 else -1)
        if 0 <= other < rows:
            o.append((s, other * TILES_Y + s % TILES_Y))
    return a, b, e, o


def select_kernel(flags, col_a, col_b, row_e, row_o, diag_e, diag_o, tag_e, tag_o):
    half = col_a.shape[0]
    toward_a = flags[5].astype(F32)
    tag_e[...] = row_e[half:]
    tag_o[...] = row_o[half:]
    e_wants_a = row_e[half + 1] == toward_a
    o_wants_a = row_o[half + 1] == toward_a

    def step(i, _):
        at = pl.ds(i * 8, 8)
        a = col_a[at]
        b = col_b[at]
        diag_e[at] = jnp.where(e_wants_a[None], a, b)
        diag_o[at] = jnp.where(o_wants_a[None], a, b)
        return 0

    lax.fori_loop(0, half // 8, step, 0)


def bucket_kernel(flags, col, back_e, back_o, tag_e, tag_o, sum_a, sum_b):
    toward_e = flags[4].astype(F32)
    toward_a = flags[5].astype(F32)
    with_a = flags[3] == 1
    from_e = tag_e[0] == -toward_e
    from_o = tag_o[0] == toward_e
    e_a = from_e & (tag_e[1] == toward_a)
    e_b = from_e & (tag_e[1] == -toward_a)
    o_a = from_o & (tag_o[1] == toward_a)
    o_b = from_o & (tag_o[1] == -toward_a)

    def step(i, _):
        at = pl.ds(i * 8, 8)
        c = col[at]
        e = back_e[at]
        o = back_o[at]
        sum_a[at] = jnp.where(with_a, c, 0.0) + jnp.where(e_a[None], e, 0.0) + jnp.where(o_a[None], o, 0.0)
        sum_b[at] = jnp.where(with_a, 0.0, c) + jnp.where(e_b[None], e, 0.0) + jnp.where(o_b[None], o, 0.0)
        return 0

    lax.fori_loop(0, col.shape[0] // 8, step, 0)


def final_kernel(flags, tile, own, same_e, same_o, tag_e, tag_o, sum_a, sum_b, out):
    toward_e = flags[4].astype(F32)
    from_e = tag_e[0] == -toward_e
    from_o = tag_o[0] == toward_e

    def step(i, _):
        at = pl.ds(i * 8, 8)
        total = own[at] + jnp.where(from_e[None], same_e[at], 0.0) + jnp.where(from_o[None], same_o[at], 0.0)
        out[at] = 2.0 * tile[at] * (total + sum_a[at] + sum_b[at])
        return 0

    lax.fori_loop(0, tile.shape[0] // 8, step, 0)


def steps(velocity, fwd_field, adj_field, aperture_anchor, source_cell, wavelet, shot_count, receiver_cell, residual):
    tile = velocity[0]
    half, depth, wide = tile.shape
    slabs = lax.axis_size("slab")
    pair_a, pair_b, pair_e, pair_o = swaps(lax.axis_size("shot"))
    to_up = [(i, i + 1) for i in range(slabs - 1)]
    to_down = [(i + 1, i) for i in range(slabs - 1)]

    def shape(*dims, dtype=F32):
        return jax.ShapeDtypeStruct(dims, dtype)

    def send(pairs, value, axis="shot"):
        return lax.ppermute(value, axis, pairs)

    def kernel(function, ins, outs, args, flops, mib=8, scratch=()):
        places = [SMEM if i == "s" else VMEM for i in ins]
        sent = tuple(SMEM if o.dtype == jnp.int32 else VMEM for o in outs)
        nbytes = sum(int(np.prod(a.shape)) * 4 for a in tuple(args) + tuple(outs))
        return pl.pallas_call(
            function,
            out_shape=tuple(outs),
            in_specs=places,
            out_specs=sent,
            scratch_shapes=list(scratch),
            compiler_params=pltpu.CompilerParams(vmem_limit_bytes=mib * 1024 * 1024),
            cost_estimate=cost(flops, nbytes),
        )(*args)

    piece = shape(half, depth, wide)
    rim_shape = shape(AX, 8, Y)
    flat = shape(FLAT, Y)
    halves = [pltpu.VMEM((FLAT, Y), BF16)] * 4
    s_high, s_low = parts_of(along_xz())
    y_high, y_low = parts_of(along_y())
    h_high, h_low = parts_of(along_halo())
    inner = tuple(jnp.asarray(m) for m in (s_high, s_low, y_high, y_low))
    rim = tuple(jnp.asarray(m) for m in (h_high, h_low))

    col_b = send(pair_b, tile)
    col_a = send(pair_a, tile)
    fwd = fwd_field[0]
    adj = adj_field[0]
    flat_fwd = fwd.reshape(FLAT, Y)
    flat_adj = adj.reshape(FLAT, Y)
    up, down, tagged, flags = kernel(
        pack_kernel, "svvv", (rim_shape, rim_shape, shape(half + 2, depth, wide), shape(8, dtype=jnp.int32)),
        (aperture_anchor, tile, fwd, adj), 1 << 20)
    row_e = send(pair_e, tagged)
    row_o = send(pair_o, tagged)
    below = send(to_up, up, "slab")
    above = send(to_down, down, "slab")
    recv = receiver_cell.shape[1]
    fwd_in1, fwd_in2, adj_in1, adj_in2 = kernel(
        functools.partial(inject_kernel, depth * slabs), "svvvv", (flat,) * 4,
        (shot_count, source_cell, wavelet[0], receiver_cell, residual[0]), 3 << 30, 12,
        [pltpu.VMEM((8, 128), F32), pltpu.VMEM((8, recv), F32), pltpu.VMEM((128, 4 * Y), BF16), pltpu.VMEM((recv, 4 * Y), BF16)])
    diag_e, diag_o, tag_e, tag_o = kernel(
        select_kernel, "svvvv", (piece, piece, shape(2, depth, wide), shape(2, depth, wide)),
        (flags, col_a, col_b, row_e, row_o), 1 << 20)
    diag_e = send(pair_e, diag_e)
    diag_o = send(pair_o, diag_o)
    lap_fwd, lap_adj = kernel(
        laplace_kernel, "vvvvvv", (flat,) * 2, (flat_fwd, flat_adj) + inner, 2 << 30, 8, halves)
    speed2, mid_fwd, mid_adj, up, down = kernel(
        advance_kernel, "s" + "v" * 17, (shape(AX, depth, Y), flat, flat, rim_shape, rim_shape),
        (flags, tile, col_a, col_b, row_e, row_o, diag_e, diag_o, lap_fwd, lap_adj, flat_fwd, flat_adj, fwd_in1, adj_in1,
         below.reshape(AX * 8, Y), above.reshape(AX * 8, Y)) + rim, 1 << 30)
    below = send(to_up, up, "slab")
    above = send(to_down, down, "slab")
    lap_fwd, lap_adj = kernel(laplace_kernel, "vvvvvv", (flat,) * 2, (mid_fwd, mid_adj) + inner, 2 << 30, 8, halves)
    own, col, row, diag = kernel(
        image_kernel, "s" + "v" * 13, (piece,) * 4,
        (flags, speed2.reshape(FLAT, Y), lap_fwd, lap_adj, flat_fwd, flat_adj, mid_fwd, mid_adj, fwd_in2, adj_in2,
         below.reshape(AX * 8, Y), above.reshape(AX * 8, Y)) + rim, 1 << 30, 8, [pltpu.VMEM((AX, depth, Y), F32)])
    back_e = send(pair_e, diag)
    back_o = send(pair_o, diag)
    sum_a, sum_b = kernel(
        bucket_kernel, "svvvvv", (piece,) * 2, (flags, col, back_e, back_o, tag_e, tag_o), 1 << 20)
    sum_b = send(pair_b, sum_b)
    sum_a = send(pair_a, sum_a)
    same_e = send(pair_e, row)
    same_o = send(pair_o, row)
    (out,) = kernel(
        final_kernel, "s" + "v" * 8, (piece,), (flags, tile, own, same_e, same_o, tag_e, tag_o, sum_a, sum_b), 1 << 20)
    return out[None]


def solution(mesh):
    placed = (
        P("shot", None, "slab", None),
        P("shot", None, "slab", None),
        P("shot", None, "slab", None),
        P("shot", None),
        P("shot", None),
        P("shot", None, None),
        P("shot"),
        P("shot", None),
        P("shot", None, None),
    )
    return jax.shard_map(steps, mesh=mesh, in_specs=placed, out_specs=P("shot", None, "slab", None), check_vma=False)
```

```python
import functools

import jax
import jax.numpy as jnp
import numpy as np
from jax import lax
from jax.experimental import pallas as pl
from jax.experimental.pallas import tpu as pltpu
from jax.sharding import PartitionSpec as P


TILES_Y = 4
SCALE = 5040.0
STENCIL = (8064.0, -1008.0, 128.0, -9.0)
CENTRE_XZ = -43008.0
CENTRE_Y = -42.0

BX = 8
Z = 16
Y = 256
Y_BITS = 8
AX = 64
ROWS = BX * Z
BLOCKS = AX // BX
FLAT = AX * Z
F32 = jnp.float32
BF16 = jnp.bfloat16
VMEM = pl.BlockSpec(memory_space=pltpu.VMEM)
SMEM = pl.BlockSpec(memory_space=pltpu.SMEM)


def weight(distance):
    distance = np.abs(distance)
    table = np.array((0.0,) + STENCIL + (0.0,))
    return table[np.minimum(distance, 5)]


def exact(matrix):
    narrow = matrix.astype(np.float32).astype(jnp.bfloat16)
    assert np.array_equal(narrow.astype(np.float64), matrix)
    return jnp.asarray(narrow)


def along_xz():
    out_x, out_z = np.divmod(np.arange(ROWS), Z)
    in_x, in_z = np.divmod(np.arange(2 * ROWS), Z)
    kinds = []
    for lead in (0, 4, 8):
        dx = out_x[:, None] - (in_x[None, :] - lead)
        dz = out_z[:, None] - in_z[None, :]
        both = np.where(dz == 0, weight(dx), 0.0) + np.where(dx == 0, weight(dz), 0.0)
        kinds.append(both + np.where((dx == 0) & (dz == 0), CENTRE_XZ, 0.0))
    return np.stack(kinds)


def along_y():
    at = np.arange(Y)
    return weight(at[:, None] - at[None, :]) + CENTRE_Y * np.eye(Y)


def along_halo():
    field, rest = np.divmod(np.arange(ROWS), BX * 8)
    out_x, out_s = np.divmod(rest, 8)
    out_z = np.where(out_s < 4, out_s, Z - 8 + out_s)
    side, rest = np.divmod(np.arange(ROWS), BX * 8)
    in_x, in_s = np.divmod(rest, 8)
    in_z = np.where(side == 0, in_s % 4 - 4, Z + in_s % 4)
    same = (out_x[:, None] == in_x[None, :]) & (field[:, None] == in_s[None, :] // 4)
    return np.where(same, weight(out_z[:, None] - in_z[None, :]), 0.0)


def dot(a, b):
    return jnp.dot(a, b, preferred_element_type=F32)


def split(value):
    high = value.astype(BF16)
    return high, (value - high.astype(F32)).astype(BF16)


def split3(value):
    high = value.astype(BF16)
    rest = value - high.astype(F32)
    middle = rest.astype(BF16)
    return high, middle, (rest - middle.astype(F32)).astype(BF16)


def cost(flops, nbytes):
    return pl.CostEstimate(flops=flops, transcendentals=0, bytes_accessed=nbytes)


def rims(fwd, adj):
    front = lax.broadcasted_iota(jnp.int32, (BX, 8, Y), 1) < 4
    top = jnp.where(front, pltpu.roll(fwd[:, 8:, :], 4, 1), adj[:, 8:, :])
    bottom = jnp.where(front, fwd[:, :8, :], pltpu.roll(adj[:, :8, :], 4, 1))
    return top, bottom


def tag_kernel(anchor, vel, tagged, flags):
    device = lax.axis_index("shot")
    home_row = device // TILES_Y
    home_col = device - home_row * TILES_Y
    part_row = home_row - anchor[0, 0]
    part_col = home_col - anchor[0, 1]
    side_row = 1 - 2 * part_row
    side_col = 1 - 2 * part_col
    toward_e = 1 - 2 * (home_row & 1)
    toward_a = 1 - 2 * (home_col & 1)
    flags[0] = part_row
    flags[1] = part_col
    flags[2] = jnp.where(side_row == toward_e, 1, 0)
    flags[3] = jnp.where(side_col == toward_a, 1, 0)
    flags[4] = toward_e
    flags[5] = toward_a
    rows = vel.shape[0]
    tagged[rows] = jnp.full(tagged.shape[1:], side_row.astype(F32))
    tagged[rows + 1] = jnp.full(tagged.shape[1:], side_col.astype(F32))

    def copy(i, _):
        at = pl.ds(i * 8, 8)
        tagged[at] = vel[at]
        return 0

    lax.fori_loop(0, rows // 8, copy, 0)


def rims_kernel(fwd, adj, up, down):
    def step(b, _):
        at = pl.ds(b * BX, BX)
        up[at], down[at] = rims(fwd[at], adj[at])
        return 0

    lax.fori_loop(0, BLOCKS, step, 0)


def inner_laplace(b, parts, xz, y):
    kind = jnp.where(b == 0, 0, jnp.where(b == BLOCKS - 1, 2, 1))
    first = jnp.clip(b * BX - 4, 0, AX - 2 * BX) * Z
    window = pl.ds(pl.multiple_of(first, 64), 2 * ROWS)
    own = pl.ds(pl.multiple_of(b * ROWS, ROWS), ROWS)
    high, middle, low = parts
    result = dot(xz[kind], low[window]) + dot(low[own], y[...])
    result = result + (dot(xz[kind], middle[window]) + dot(middle[own], y[...]))
    return result + (dot(xz[kind], high[window]) + dot(high[own], y[...]))


def split_all(field, parts):
    def step(b, _):
        at = pl.ds(pl.multiple_of(b * ROWS, ROWS), ROWS)
        parts[0][at], parts[1][at], parts[2][at] = split3(field[at])
        return 0

    lax.fori_loop(0, BLOCKS, step, 0)


def table_of(cells, amounts, first_layer, total_depth, table):
    count = cells.shape[1]
    column = cells >> Y_BITS
    cell_x = ((column.astype(F32) + 0.5) * (1.0 / total_depth)).astype(jnp.int32)
    cell_z = column - cell_x * total_depth - first_layer
    inside = (cell_z >= 0) & (cell_z < Z)
    table[...] = jnp.full(table.shape, -1.0, F32)
    table[0:1, 0:count] = jnp.where(inside, cell_x * Z + cell_z, -1).astype(F32)
    table[1:2, 0:count] = (cells & (Y - 1)).astype(F32)
    table[2:3, 0:count] = amounts[0]
    table[3:4, 0:count] = amounts[1]


def columns_of(points, n, columns):
    def step(i, _):
        at = pl.ds(pl.multiple_of(i * 128, 128), 128)
        part = points[:, at].T
        here = lax.broadcasted_iota(jnp.int32, (128, Y), 1) == part[:, 1:2].astype(jnp.int32)
        high, low = split(part[:, 2 + n : 3 + n])
        columns[at, :Y] = jnp.where(here, high.astype(F32), 0.0).astype(BF16)
        columns[at, Y:] = jnp.where(here, low.astype(F32), 0.0).astype(BF16)
        return 0

    lax.fori_loop(0, points.shape[1] // 128, step, 0)


def injected(b, points, columns):
    rows = lax.broadcasted_iota(jnp.int32, (ROWS, points.shape[1]), 0) + b * ROWS
    hot = jnp.where(rows == points[0:1, :].astype(jnp.int32), 1.0, 0.0).astype(BF16)
    both = dot(hot, columns[...])
    return both[:, :Y] + both[:, Y:]


def inject_kernel(total_depth, n, shot_count, source_cell, wavelet, receiver_cell, residual, after, fwd_in, adj_in,
                  shots, receivers, shot_columns, receiver_columns):
    first_layer = lax.axis_index("slab") * Z
    active = lax.broadcasted_iota(jnp.int32, source_cell.shape, 1) < shot_count[0]
    waves = [jnp.where(active, wavelet[i : i + 1, :], 0.0) for i in range(2)]
    table_of(source_cell[...], waves, first_layer, total_depth, shots)
    table_of(receiver_cell[...], [residual[1:2, :], residual[0:1, :]], first_layer, total_depth, receivers)
    columns_of(shots, n, shot_columns)
    columns_of(receivers, n, receiver_columns)

    def step(b, _):
        at = pl.ds(pl.multiple_of(b * ROWS, ROWS), ROWS)
        fwd_in[at] = injected(b, shots, shot_columns)
        adj_in[at] = injected(b, receivers, receiver_columns)
        return 0

    lax.fori_loop(0, BLOCKS, step, 0)


def laplace_kernel(fwd, adj, xz, y, lap_fwd, lap_adj, f0, f1, f2, a0, a1, a2):
    split_all(fwd, (f0, f1, f2))
    split_all(adj, (a0, a1, a2))

    def step(b, _):
        at = pl.ds(pl.multiple_of(b * ROWS, ROWS), ROWS)
        lap_fwd[at] = inner_laplace(b, (f0, f1, f2), xz, y)
        lap_adj[at] = inner_laplace(b, (a0, a1, a2), xz, y)
        return 0

    lax.fori_loop(0, BLOCKS, step, 0)


def halo_part(b, below, above, halo):
    at = pl.ds(pl.multiple_of(b * (ROWS // 2), ROWS // 2), ROWS // 2)
    high, middle, low = split3(jnp.concatenate([below[at], above[at]], 0))
    both = dot(halo[...], low) + dot(halo[...], middle) + dot(halo[...], high)
    front = lax.broadcasted_iota(jnp.int32, (BX, 8, Y), 1) < 4
    fields = []
    for part in (both[: ROWS // 2], both[ROWS // 2 :]):
        part = part.reshape(BX, 8, Y)
        fields.append(jnp.concatenate([jnp.where(front, part, 0.0), jnp.where(front, 0.0, part)], 1).reshape(ROWS, Y))
    return fields


def advance_kernel(flags, own, col_a, col_b, row_e, row_o, diag_e, diag_o, lap_fwd, lap_adj, fwd, adj, fwd_in, adj_in,
                   below, above, halo, speed2, mid_fwd, mid_adj, up, down):
    half = own.shape[0]
    wide = own.shape[2]
    with_e = flags[2] == 1
    with_a = flags[3] == 1
    row_at = flags[0] * half
    row_to = (1 - flags[0]) * half
    col_at = pl.ds(pl.multiple_of(flags[1] * wide, wide), wide)
    col_to = pl.ds(pl.multiple_of((1 - flags[1]) * wide, wide), wide)

    def assemble(i, _):
        at = pl.ds(i * 8, 8)
        near = pl.ds(row_at + i * 8, 8)
        far = pl.ds(row_to + i * 8, 8)
        speed = own[at]
        speed2[near, :, col_at] = speed * speed * (1.0 / SCALE)
        speed = jnp.where(with_a, col_a[at], col_b[at])
        speed2[near, :, col_to] = speed * speed * (1.0 / SCALE)
        speed = jnp.where(with_e, row_e[at], row_o[at])
        speed2[far, :, col_at] = speed * speed * (1.0 / SCALE)
        speed = jnp.where(with_e, diag_e[at], diag_o[at])
        speed2[far, :, col_to] = speed * speed * (1.0 / SCALE)
        return 0

    lax.fori_loop(0, half // 8, assemble, 0)

    def step(b, _):
        at = pl.ds(pl.multiple_of(b * ROWS, ROWS), ROWS)
        blk = pl.ds(b * BX, BX)
        halo_fwd, halo_adj = halo_part(b, below, above, halo)
        c = speed2[blk].reshape(ROWS, Y)
        new_fwd = fwd[at] + (c * (lap_fwd[at] + halo_fwd) + fwd_in[at])
        new_adj = adj[at] + (c * (lap_adj[at] + halo_adj) + adj_in[at])
        mid_fwd[at] = new_fwd
        mid_adj[at] = new_adj
        up[blk], down[blk] = rims(new_fwd.reshape(BX, Z, Y), new_adj.reshape(BX, Z, Y))
        return 0

    lax.fori_loop(0, BLOCKS, step, 0)


def image_kernel(flags, speed2, lap_fwd, lap_adj, fwd, adj, mid_fwd, mid_adj, fwd_in, adj_in, below, above, halo,
                 own, col, row, diag, image):
    def step(b, _):
        at = pl.ds(pl.multiple_of(b * ROWS, ROWS), ROWS)
        halo_fwd, halo_adj = halo_part(b, below, above, halo)
        c = speed2[at]
        second_fwd = c * (lap_fwd[at] + halo_fwd) + fwd_in[at]
        second_adj = c * (lap_adj[at] + halo_adj) + adj_in[at]
        later = mid_adj[at]
        earlier = 2.0 * later - adj[at] + second_adj
        imaged = earlier * (mid_fwd[at] - fwd[at]) + later * second_fwd
        image[pl.ds(b * BX, BX)] = imaged.reshape(BX, Z, Y)
        return 0

    lax.fori_loop(0, BLOCKS, step, 0)
    half = own.shape[0]
    wide = own.shape[2]
    row_at = flags[0] * half
    row_to = (1 - flags[0]) * half
    col_at = pl.ds(pl.multiple_of(flags[1] * wide, wide), wide)
    col_to = pl.ds(pl.multiple_of((1 - flags[1]) * wide, wide), wide)

    def hand_out(i, _):
        at = pl.ds(i * 8, 8)
        near = pl.ds(row_at + i * 8, 8)
        far = pl.ds(row_to + i * 8, 8)
        own[at] = image[near, :, col_at]
        col[at] = image[near, :, col_to]
        row[at] = image[far, :, col_at]
        diag[at] = image[far, :, col_to]
        return 0

    lax.fori_loop(0, half // 8, hand_out, 0)


def swaps(count):
    rows = count // TILES_Y
    a = [(s, s ^ 1) for s in range(count)]
    b = [(s, s + 1) if s % TILES_Y == 1 else (s, s - 1) for s in range(count) if s % TILES_Y in (1, 2)]
    e = [(s, s + TILES_Y if (s // TILES_Y) % 2 == 0 else s - TILES_Y) for s in range(count)]
    o = []
    for s in range(count):
        other = s // TILES_Y + (1 if (s // TILES_Y) % 2 else -1)
        if 0 <= other < rows:
            o.append((s, other * TILES_Y + s % TILES_Y))
    return a, b, e, o


def select_kernel(flags, col_a, col_b, row_e, row_o, diag_e, diag_o, tag_e, tag_o):
    half = col_a.shape[0]
    toward_a = flags[5].astype(F32)
    tag_e[...] = row_e[half:]
    tag_o[...] = row_o[half:]
    e_wants_a = row_e[half + 1] == toward_a
    o_wants_a = row_o[half + 1] == toward_a

    def step(i, _):
        at = pl.ds(i * 8, 8)
        a = col_a[at]
        b = col_b[at]
        diag_e[at] = jnp.where(e_wants_a[None], a, b)
        diag_o[at] = jnp.where(o_wants_a[None], a, b)
        return 0

    lax.fori_loop(0, half // 8, step, 0)


def bucket_kernel(flags, col, back_e, back_o, tag_e, tag_o, sum_a, sum_b):
    toward_e = flags[4].astype(F32)
    toward_a = flags[5].astype(F32)
    with_a = flags[3] == 1
    from_e = tag_e[0] == -toward_e
    from_o = tag_o[0] == toward_e
    e_a = from_e & (tag_e[1] == toward_a)
    e_b = from_e & (tag_e[1] == -toward_a)
    o_a = from_o & (tag_o[1] == toward_a)
    o_b = from_o & (tag_o[1] == -toward_a)

    def step(i, _):
        at = pl.ds(i * 8, 8)
        c = col[at]
        e = back_e[at]
        o = back_o[at]
        sum_a[at] = jnp.where(with_a, c, 0.0) + jnp.where(e_a[None], e, 0.0) + jnp.where(o_a[None], o, 0.0)
        sum_b[at] = jnp.where(with_a, 0.0, c) + jnp.where(e_b[None], e, 0.0) + jnp.where(o_b[None], o, 0.0)
        return 0

    lax.fori_loop(0, col.shape[0] // 8, step, 0)


def final_kernel(flags, tile, own, same_e, same_o, tag_e, tag_o, sum_a, sum_b, out):
    toward_e = flags[4].astype(F32)
    from_e = tag_e[0] == -toward_e
    from_o = tag_o[0] == toward_e

    def step(i, _):
        at = pl.ds(i * 8, 8)
        total = own[at] + jnp.where(from_e[None], same_e[at], 0.0) + jnp.where(from_o[None], same_o[at], 0.0)
        out[at] = 2.0 * tile[at] * (total + sum_a[at] + sum_b[at])
        return 0

    lax.fori_loop(0, tile.shape[0] // 8, step, 0)


def steps(velocity, fwd_field, adj_field, aperture_anchor, source_cell, wavelet, shot_count, receiver_cell, residual):
    tile = velocity[0]
    half, depth, wide = tile.shape
    slabs = lax.axis_size("slab")
    pair_a, pair_b, pair_e, pair_o = swaps(lax.axis_size("shot"))
    to_up = [(i, i + 1) for i in range(slabs - 1)]
    to_down = [(i + 1, i) for i in range(slabs - 1)]

    def shape(*dims, dtype=F32):
        return jax.ShapeDtypeStruct(dims, dtype)

    def send(pairs, value, axis="shot"):
        return lax.ppermute(value, axis, pairs)

    def kernel(function, ins, outs, args, flops, mib=8, scratch=()):
        places = [SMEM if i == "s" else VMEM for i in ins]
        sent = tuple(SMEM if o.dtype == jnp.int32 else VMEM for o in outs)
        nbytes = sum(int(np.prod(a.shape)) * 4 for a in tuple(args) + tuple(outs))
        return pl.pallas_call(
            function,
            out_shape=tuple(outs),
            in_specs=places,
            out_specs=sent,
            scratch_shapes=list(scratch),
            compiler_params=pltpu.CompilerParams(vmem_limit_bytes=mib * 1024 * 1024),
            cost_estimate=cost(flops, nbytes),
        )(*args)

    piece = shape(half, depth, wide)
    rim_shape = shape(AX, 8, Y)
    flat = shape(FLAT, Y)
    parts = [pltpu.VMEM((FLAT, Y), BF16)] * 6
    inner = (exact(along_xz()), exact(along_y()))
    rim = (exact(along_halo()),)

    col_b = send(pair_b, tile)
    col_a = send(pair_a, tile)
    fwd = fwd_field[0]
    adj = adj_field[0]
    flat_fwd = fwd.reshape(FLAT, Y)
    flat_adj = adj.reshape(FLAT, Y)
    tagged, flags = kernel(
        tag_kernel, "sv", (shape(half + 2, depth, wide), shape(8, dtype=jnp.int32)), (aperture_anchor, tile), 1 << 20)
    row_e = send(pair_e, tagged)
    row_o = send(pair_o, tagged)
    up, down = kernel(rims_kernel, "vv", (rim_shape, rim_shape), (fwd, adj), 1 << 20)
    below = send(to_up, up, "slab")
    above = send(to_down, down, "slab")
    recv = receiver_cell.shape[1]

    def inject(n, after):
        return kernel(
            functools.partial(inject_kernel, depth * slabs, n), "svvvvs", (flat,) * 2,
            (shot_count, source_cell, wavelet[0], receiver_cell, residual[0], after), 2 << 30, 12,
            [pltpu.VMEM((8, 128), F32), pltpu.VMEM((8, recv), F32), pltpu.VMEM((128, 2 * Y), BF16), pltpu.VMEM((recv, 2 * Y), BF16)])

    fwd_in1, adj_in1 = inject(0, flags)
    diag_e, diag_o, tag_e, tag_o = kernel(
        select_kernel, "svvvv", (piece, piece, shape(2, depth, wide), shape(2, depth, wide)),
        (flags, col_a, col_b, row_e, row_o), 1 << 20)
    diag_e = send(pair_e, diag_e)
    diag_o = send(pair_o, diag_o)
    lap_fwd, lap_adj = kernel(
        laplace_kernel, "vvvv", (flat,) * 2, (flat_fwd, flat_adj) + inner, 2 << 30, 8, parts)
    speed2, mid_fwd, mid_adj, up, down = kernel(
        advance_kernel, "s" + "v" * 16, (shape(AX, depth, Y), flat, flat, rim_shape, rim_shape),
        (flags, tile, col_a, col_b, row_e, row_o, diag_e, diag_o, lap_fwd, lap_adj, flat_fwd, flat_adj, fwd_in1, adj_in1,
         below.reshape(AX * 8, Y), above.reshape(AX * 8, Y)) + rim, 1 << 30)
    below = send(to_up, up, "slab")
    above = send(to_down, down, "slab")
    lap_fwd, lap_adj = kernel(laplace_kernel, "vvvv", (flat,) * 2, (mid_fwd, mid_adj) + inner, 2 << 30, 8, parts)
    fwd_in2, adj_in2 = inject(1, flags)
    own, col, row, diag = kernel(
        image_kernel, "s" + "v" * 12, (piece,) * 4,
        (flags, speed2.reshape(FLAT, Y), lap_fwd, lap_adj, flat_fwd, flat_adj, mid_fwd, mid_adj, fwd_in2, adj_in2,
         below.reshape(AX * 8, Y), above.reshape(AX * 8, Y)) + rim, 1 << 30, 8, [pltpu.VMEM((AX, depth, Y), F32)])
    back_e = send(pair_e, diag)
    back_o = send(pair_o, diag)
    sum_a, sum_b = kernel(
        bucket_kernel, "svvvvv", (piece,) * 2, (flags, col, back_e, back_o, tag_e, tag_o), 1 << 20)
    sum_b = send(pair_b, sum_b)
    sum_a = send(pair_a, sum_a)
    same_e = send(pair_e, row)
    same_o = send(pair_o, row)
    (out,) = kernel(
        final_kernel, "s" + "v" * 8, (piece,), (flags, tile, own, same_e, same_o, tag_e, tag_o, sum_a, sum_b), 1 << 20)
    return out[None]


def solution(mesh):
    placed = (
        P("shot", None, "slab", None),
        P("shot", None, "slab", None),
        P("shot", None, "slab", None),
        P("shot", None),
        P("shot", None),
        P("shot", None, None),
        P("shot"),
        P("shot", None),
        P("shot", None, None),
    )
    return jax.shard_map(steps, mesh=mesh, in_specs=placed, out_specs=P("shot", None, "slab", None), check_vma=False)
```

```python
import functools

import jax
import jax.numpy as jnp
import numpy as np
from jax import lax
from jax.experimental import pallas as pl
from jax.experimental.pallas import tpu as pltpu
from jax.sharding import PartitionSpec as P


TILES_Y = 4
SCALE = 5040.0
STENCIL = (8064.0, -1008.0, 128.0, -9.0)
CENTRE_XZ = -43008.0
CENTRE_Y = -42.0

BX = 8
Z = 16
Y = 256
Y_BITS = 8
AX = 64
ROWS = BX * Z
BLOCKS = AX // BX
HOT = 512
FLAT = AX * Z
F32 = jnp.float32
BF16 = jnp.bfloat16
VMEM = pl.BlockSpec(memory_space=pltpu.VMEM)
SMEM = pl.BlockSpec(memory_space=pltpu.SMEM)
HBM = pl.BlockSpec(memory_space=pltpu.HBM)
PIECES = 4


def weight(distance):
    distance = np.abs(distance)
    table = np.array((0.0,) + STENCIL + (0.0,))
    return table[np.minimum(distance, 5)]


def exact(matrix):
    narrow = matrix.astype(np.float32).astype(jnp.bfloat16)
    assert np.array_equal(narrow.astype(np.float64), matrix)
    return jnp.asarray(narrow)


def along_xz():
    out_x, out_z = np.divmod(np.arange(ROWS), Z)
    in_x, in_z = np.divmod(np.arange(2 * ROWS), Z)
    kinds = []
    for lead in (0, 4, 8):
        dx = out_x[:, None] - (in_x[None, :] - lead)
        dz = out_z[:, None] - in_z[None, :]
        both = np.where(dz == 0, weight(dx), 0.0) + np.where(dx == 0, weight(dz), 0.0)
        kinds.append(both + np.where((dx == 0) & (dz == 0), CENTRE_XZ, 0.0))
    return np.stack(kinds)


def along_y():
    at = np.arange(Y)
    return weight(at[:, None] - at[None, :]) + CENTRE_Y * np.eye(Y)


def along_halo():
    field, rest = np.divmod(np.arange(ROWS), BX * 8)
    out_x, out_s = np.divmod(rest, 8)
    out_z = np.where(out_s < 4, out_s, Z - 8 + out_s)
    side, rest = np.divmod(np.arange(ROWS), BX * 8)
    in_x, in_s = np.divmod(rest, 8)
    in_z = np.where(side == 0, in_s % 4 - 4, Z + in_s % 4)
    same = (out_x[:, None] == in_x[None, :]) & (field[:, None] == in_s[None, :] // 4)
    return np.where(same, weight(out_z[:, None] - in_z[None, :]), 0.0)


def dot(a, b):
    return jnp.dot(a, b, preferred_element_type=F32)


def split3(value):
    high = value.astype(BF16)
    rest = value - high.astype(F32)
    middle = rest.astype(BF16)
    return high, middle, (rest - middle.astype(F32)).astype(BF16)


def cost(flops, nbytes):
    return pl.CostEstimate(flops=flops, transcendentals=0, bytes_accessed=nbytes)


def rims(fwd, adj):
    front = lax.broadcasted_iota(jnp.int32, (BX, 8, Y), 1) < 4
    top = jnp.where(front, pltpu.roll(fwd[:, 8:, :], 4, 1), adj[:, 8:, :])
    bottom = jnp.where(front, fwd[:, :8, :], pltpu.roll(adj[:, :8, :], 4, 1))
    return top, bottom


def load_kernel(anchor, vel_hbm, fwd_hbm, adj_hbm, tagged, fwd, adj, up, down, flags, sems):
    rows = vel_hbm.shape[0]
    tile_copy = pltpu.make_async_copy(vel_hbm, tagged.at[pl.ds(0, rows)], sems.at[2 * PIECES])
    size = AX // PIECES
    copies = []
    for n, (source, target) in enumerate(((fwd_hbm, fwd), (adj_hbm, adj))):
        for i in range(PIECES):
            at = pl.ds(i * size, size)
            copies.append(pltpu.make_async_copy(source.at[at], target.at[at], sems.at[n * PIECES + i]))
    for copy in copies:
        copy.start()
    tile_copy.start()
    device = lax.axis_index("shot")
    home_row = device // TILES_Y
    home_col = device - home_row * TILES_Y
    part_row = home_row - anchor[0, 0]
    part_col = home_col - anchor[0, 1]
    side_row = 1 - 2 * part_row
    side_col = 1 - 2 * part_col
    toward_e = 1 - 2 * (home_row & 1)
    toward_a = 1 - 2 * (home_col & 1)
    flags[0] = part_row
    flags[1] = part_col
    flags[2] = jnp.where(side_row == toward_e, 1, 0)
    flags[3] = jnp.where(side_col == toward_a, 1, 0)
    flags[4] = toward_e
    flags[5] = toward_a
    tagged[rows] = jnp.full(tagged.shape[1:], side_row.astype(F32))
    tagged[rows + 1] = jnp.full(tagged.shape[1:], side_col.astype(F32))

    for copy in copies:
        copy.wait()

    def step(b, _):
        at = pl.ds(b * BX, BX)
        up[at], down[at] = rims(fwd[at], adj[at])
        return 0

    lax.fori_loop(0, BLOCKS, step, 0)
    tile_copy.wait()


def inner_laplace(b, parts, xz, y):
    kind = jnp.where(b == 0, 0, jnp.where(b == BLOCKS - 1, 2, 1))
    first = jnp.clip(b * BX - 4, 0, AX - 2 * BX) * Z
    window = pl.ds(pl.multiple_of(first, 64), 2 * ROWS)
    own = pl.ds(pl.multiple_of(b * ROWS, ROWS), ROWS)
    high, middle, low = parts
    result = dot(xz[kind], low[window]) + dot(low[own], y[...])
    result = result + (dot(xz[kind], middle[window]) + dot(middle[own], y[...]))
    return result + (dot(xz[kind], high[window]) + dot(high[own], y[...]))


def split_all(field, parts):
    def step(b, _):
        at = pl.ds(pl.multiple_of(b * ROWS, ROWS), ROWS)
        parts[0][at], parts[1][at], parts[2][at] = split3(field[at])
        return 0

    lax.fori_loop(0, BLOCKS, step, 0)


def table_of(cells, amounts, first_layer, total_depth, table):
    count = cells.shape[1]
    column = cells >> Y_BITS
    cell_x = ((column.astype(F32) + 0.5) * (1.0 / total_depth)).astype(jnp.int32)
    cell_z = column - cell_x * total_depth - first_layer
    inside = (cell_z >= 0) & (cell_z < Z)
    table[...] = jnp.full(table.shape, -1.0, F32)
    table[0:1, 0:count] = jnp.where(inside, cell_x * Z + cell_z, -1).astype(F32)
    table[1:2, 0:count] = (cells & (Y - 1)).astype(F32)
    table[2:3, 0:count] = amounts[0]
    table[3:4, 0:count] = amounts[1]


def ones_of(points, ones):
    def step(i, _):
        at = pl.ds(pl.multiple_of(i * 128, 128), 128)
        place = jnp.broadcast_to(points[1:2, at], (8, 128)).T[:, 0:1].astype(jnp.int32)
        here = lax.broadcasted_iota(jnp.int32, (128, Y), 1) == place
        ones[at] = jnp.where(here, 1.0, 0.0).astype(BF16)
        return 0

    lax.fori_loop(0, points.shape[1] // 128, step, 0)


def hot_rows(b, points, n, hot):
    count = points.shape[1]
    amount = points[2 + n : 3 + n, :]
    part = amount.astype(BF16).astype(F32)
    rest = (amount - part).astype(BF16).astype(F32)
    rows = points[0:1, :].astype(jnp.int32)
    for i in range(HOT // 128):
        hit = lax.broadcasted_iota(jnp.int32, (128, count), 0) + (b * HOT + i * 128) == rows
        hot[pl.ds(i * 128, 128)] = jnp.where(hit, part, 0.0).astype(BF16)
        hot[pl.ds(HOT + i * 128, 128)] = jnp.where(hit, rest, 0.0).astype(BF16)


def inject_all(n, shots, receivers, shot_ones, receiver_ones, fwd_in, adj_in, shot_hot, hot):
    def step(b, _):
        at = pl.ds(pl.multiple_of(b * HOT, HOT), HOT)
        for points, ones, rows, field in ((shots, shot_ones, shot_hot, fwd_in), (receivers, receiver_ones, hot, adj_in)):
            hot_rows(b, points, n, rows)
            both = dot(rows[...], ones[...])
            field[at] = both[:HOT] + both[HOT:]
        return 0

    lax.fori_loop(0, FLAT // HOT, step, 0)


def inject_kernel(total_depth, shot_count, source_cell, wavelet, receiver_cell, residual,
                  fwd_in, adj_in, shots, receivers, shot_ones, receiver_ones, *hot):
    first_layer = lax.axis_index("slab") * Z
    active = lax.broadcasted_iota(jnp.int32, source_cell.shape, 1) < shot_count[0]
    waves = [jnp.where(active, wavelet[i : i + 1, :], 0.0) for i in range(2)]
    table_of(source_cell[...], waves, first_layer, total_depth, shots)
    table_of(receiver_cell[...], [residual[1:2, :], residual[0:1, :]], first_layer, total_depth, receivers)
    ones_of(shots, shot_ones)
    ones_of(receivers, receiver_ones)
    inject_all(0, shots, receivers, shot_ones, receiver_ones, fwd_in, adj_in, *hot)


def inject_again_kernel(shots, receivers, shot_ones, receiver_ones, fwd_in, adj_in, *hot):
    inject_all(1, shots, receivers, shot_ones, receiver_ones, fwd_in, adj_in, *hot)


def laplace_kernel(fwd, adj, xz, y, lap_fwd, lap_adj, f0, f1, f2, a0, a1, a2):
    split_all(fwd, (f0, f1, f2))
    split_all(adj, (a0, a1, a2))

    def step(b, _):
        at = pl.ds(pl.multiple_of(b * ROWS, ROWS), ROWS)
        lap_fwd[at] = inner_laplace(b, (f0, f1, f2), xz, y)
        lap_adj[at] = inner_laplace(b, (a0, a1, a2), xz, y)
        return 0

    lax.fori_loop(0, BLOCKS, step, 0)


def halo_part(b, below, above, halo, both):
    at = pl.ds(pl.multiple_of(b * (ROWS // 2), ROWS // 2), ROWS // 2)
    high, middle, low = split3(jnp.concatenate([below[at], above[at]], 0))
    both[...] = dot(halo[...], low) + dot(halo[...], middle) + dot(halo[...], high)


def halo_of(i, both):
    front = lax.broadcasted_iota(jnp.int32, (8, Y), 0) < 4
    fields = []
    for field in (0, 1):
        part = both[pl.ds(field * (ROWS // 2) + i * 8, 8)]
        fields.append(jnp.concatenate([jnp.where(front, part, 0.0), jnp.where(front, 0.0, part)], 0))
    return fields


def advance_kernel(flags, own, col_a, col_b, row_e, row_o, diag_e, diag_o, lap_fwd, lap_adj, fwd, adj, fwd_in, adj_in,
                   below, above, halo, speed2, mid_fwd, mid_adj, up, down, both):
    half = col_a.shape[0]
    wide = own.shape[2]
    with_e = flags[2] == 1
    with_a = flags[3] == 1
    row_at = flags[0] * half
    row_to = (1 - flags[0]) * half
    col_at = pl.ds(pl.multiple_of(flags[1] * wide, wide), wide)
    col_to = pl.ds(pl.multiple_of((1 - flags[1]) * wide, wide), wide)

    def assemble(i, _):
        at = pl.ds(i * 8, 8)
        near = pl.ds(row_at + i * 8, 8)
        far = pl.ds(row_to + i * 8, 8)
        speed = own[at]
        speed2[near, :, col_at] = speed * speed * (1.0 / SCALE)
        speed = jnp.where(with_a, col_a[at], col_b[at])
        speed2[near, :, col_to] = speed * speed * (1.0 / SCALE)
        speed = jnp.where(with_e, row_e[at], row_o[at])
        speed2[far, :, col_at] = speed * speed * (1.0 / SCALE)
        speed = jnp.where(with_e, diag_e[at], diag_o[at])
        speed2[far, :, col_to] = speed * speed * (1.0 / SCALE)
        return 0

    lax.fori_loop(0, half // 8, assemble, 0)

    def step(b, _):
        halo_part(b, below, above, halo, both)
        front = lax.broadcasted_iota(jnp.int32, (8, Y), 0) < 4
        for i in range(BX):
            x = b * BX + i
            at = pl.ds(pl.multiple_of(x * Z, Z), Z)
            halo_fwd, halo_adj = halo_of(i, both)
            c = speed2[x]
            new_fwd = fwd[at] + (c * (lap_fwd[at] + halo_fwd) + fwd_in[at])
            new_adj = adj[at] + (c * (lap_adj[at] + halo_adj) + adj_in[at])
            mid_fwd[at] = new_fwd
            mid_adj[at] = new_adj
            up[x] = jnp.where(front, pltpu.roll(new_fwd[8:], 4, 0), new_adj[8:])
            down[x] = jnp.where(front, new_fwd[:8], pltpu.roll(new_adj[:8], 4, 0))
        return 0

    lax.fori_loop(0, BLOCKS, step, 0)


def image_kernel(flags, speed2, lap_fwd, lap_adj, fwd, adj, mid_fwd, mid_adj, fwd_in, adj_in, below, above, halo,
                 own, col, row, diag, image, both):
    def step(b, _):
        halo_part(b, below, above, halo, both)
        for i in range(BX):
            x = b * BX + i
            at = pl.ds(pl.multiple_of(x * Z, Z), Z)
            halo_fwd, halo_adj = halo_of(i, both)
            c = speed2[at]
            second_fwd = c * (lap_fwd[at] + halo_fwd) + fwd_in[at]
            second_adj = c * (lap_adj[at] + halo_adj) + adj_in[at]
            later = mid_adj[at]
            earlier = 2.0 * later - adj[at] + second_adj
            image[x] = earlier * (mid_fwd[at] - fwd[at]) + later * second_fwd
        return 0

    lax.fori_loop(0, BLOCKS, step, 0)
    half = own.shape[0]
    wide = own.shape[2]
    row_at = flags[0] * half
    row_to = (1 - flags[0]) * half
    col_at = pl.ds(pl.multiple_of(flags[1] * wide, wide), wide)
    col_to = pl.ds(pl.multiple_of((1 - flags[1]) * wide, wide), wide)

    def hand_out(i, _):
        at = pl.ds(i * 8, 8)
        near = pl.ds(row_at + i * 8, 8)
        far = pl.ds(row_to + i * 8, 8)
        own[at] = image[near, :, col_at]
        col[at] = image[near, :, col_to]
        row[at] = image[far, :, col_at]
        diag[at] = image[far, :, col_to]
        return 0

    lax.fori_loop(0, half // 8, hand_out, 0)


def swaps(count):
    rows = count // TILES_Y
    a = [(s, s ^ 1) for s in range(count)]
    b = [(s, s + 1) if s % TILES_Y == 1 else (s, s - 1) for s in range(count) if s % TILES_Y in (1, 2)]
    e = [(s, s + TILES_Y if (s // TILES_Y) % 2 == 0 else s - TILES_Y) for s in range(count)]
    o = []
    for s in range(count):
        other = s // TILES_Y + (1 if (s // TILES_Y) % 2 else -1)
        if 0 <= other < rows:
            o.append((s, other * TILES_Y + s % TILES_Y))
    return a, b, e, o


def select_kernel(flags, col_a, col_b, row_e, row_o, diag_e, diag_o, tag_e, tag_o):
    half = col_a.shape[0]
    toward_a = flags[5].astype(F32)
    tag_e[...] = row_e[half:]
    tag_o[...] = row_o[half:]
    e_wants_a = row_e[half + 1] == toward_a
    o_wants_a = row_o[half + 1] == toward_a

    def step(i, _):
        at = pl.ds(i * 8, 8)
        a = col_a[at]
        b = col_b[at]
        diag_e[at] = jnp.where(e_wants_a[None], a, b)
        diag_o[at] = jnp.where(o_wants_a[None], a, b)
        return 0

    lax.fori_loop(0, half // 8, step, 0)


def bucket_kernel(flags, col, back_e, back_o, tag_e, tag_o, sum_a, sum_b):
    toward_e = flags[4].astype(F32)
    toward_a = flags[5].astype(F32)
    with_a = flags[3] == 1
    from_e = tag_e[0] == -toward_e
    from_o = tag_o[0] == toward_e
    e_a = from_e & (tag_e[1] == toward_a)
    e_b = from_e & (tag_e[1] == -toward_a)
    o_a = from_o & (tag_o[1] == toward_a)
    o_b = from_o & (tag_o[1] == -toward_a)

    def step(i, _):
        at = pl.ds(i * 8, 8)
        c = col[at]
        e = back_e[at]
        o = back_o[at]
        sum_a[at] = jnp.where(with_a, c, 0.0) + jnp.where(e_a[None], e, 0.0) + jnp.where(o_a[None], o, 0.0)
        sum_b[at] = jnp.where(with_a, 0.0, c) + jnp.where(e_b[None], e, 0.0) + jnp.where(o_b[None], o, 0.0)
        return 0

    lax.fori_loop(0, col.shape[0] // 8, step, 0)


def near_kernel(flags, tile, own, same_e, same_o, tag_e, tag_o, sum_a, near, twice):
    toward_e = flags[4].astype(F32)
    from_e = tag_e[0] == -toward_e
    from_o = tag_o[0] == toward_e

    def step(i, _):
        at = pl.ds(i * 8, 8)
        total = own[at] + jnp.where(from_e[None], same_e[at], 0.0) + jnp.where(from_o[None], same_o[at], 0.0)
        double = 2.0 * tile[at]
        twice[at] = double
        near[at] = double * (total + sum_a[at])
        return 0

    lax.fori_loop(0, own.shape[0] // 8, step, 0)


def steps(velocity, fwd_field, adj_field, aperture_anchor, source_cell, wavelet, shot_count, receiver_cell, residual):
    tile = velocity[0]
    half, depth, wide = tile.shape
    slabs = lax.axis_size("slab")
    pair_a, pair_b, pair_e, pair_o = swaps(lax.axis_size("shot"))
    to_up = [(i, i + 1) for i in range(slabs - 1)]
    to_down = [(i + 1, i) for i in range(slabs - 1)]

    def shape(*dims, dtype=F32):
        return jax.ShapeDtypeStruct(dims, dtype)

    def send(pairs, value, axis="shot"):
        return lax.ppermute(value, axis, pairs)

    def kernel(function, ins, outs, args, flops, mib=8, scratch=()):
        places = [{"s": SMEM, "h": HBM, "v": VMEM}[i] for i in ins]
        sent = tuple(SMEM if o.dtype == jnp.int32 else VMEM for o in outs)
        nbytes = sum(int(np.prod(a.shape)) * 4 for a in tuple(args) + tuple(outs))
        return pl.pallas_call(
            function,
            out_shape=tuple(outs),
            in_specs=places,
            out_specs=sent,
            scratch_shapes=list(scratch),
            compiler_params=pltpu.CompilerParams(vmem_limit_bytes=mib * 1024 * 1024),
            cost_estimate=cost(flops, nbytes),
        )(*args)

    piece = shape(half, depth, wide)
    rim_shape = shape(AX, 8, Y)
    flat = shape(FLAT, Y)
    parts = [pltpu.VMEM((FLAT, Y), BF16)] * 6
    both = [pltpu.VMEM((ROWS, Y), F32)]
    inner = (exact(along_xz()), exact(along_y()))
    rim = (exact(along_halo()),)

    col_b = send(pair_b, tile)
    col_a = send(pair_a, tile)
    field = shape(AX, depth, Y)
    tagged, fwd, adj, up, down, flags = kernel(
        load_kernel, "shhh",
        (shape(half + 2, depth, wide), field, field, rim_shape, rim_shape, shape(8, dtype=jnp.int32)),
        (aperture_anchor, tile, fwd_field[0], adj_field[0]), 1 << 20, 50, [pltpu.SemaphoreType.DMA((2 * PIECES + 1,))])
    flat_fwd = fwd.reshape(FLAT, Y)
    flat_adj = adj.reshape(FLAT, Y)
    row_e = send(pair_e, tagged)
    row_o = send(pair_o, tagged)
    below = send(to_up, up, "slab")
    above = send(to_down, down, "slab")
    recv = receiver_cell.shape[1]

    hot = [pltpu.VMEM((2 * HOT, n), BF16) for n in (128, recv)]
    ones = (shape(128, Y, dtype=BF16), shape(recv, Y, dtype=BF16))
    fwd_in1, adj_in1, *points = kernel(
        functools.partial(inject_kernel, depth * slabs), "svvvv",
        (flat, flat, shape(8, 128), shape(8, recv)) + ones,
        (shot_count, source_cell, wavelet[0], receiver_cell, residual[0]), 2 << 30, 12, hot)
    diag_e, diag_o, tag_e, tag_o = kernel(
        select_kernel, "svvvv", (piece, piece, shape(2, depth, wide), shape(2, depth, wide)),
        (flags, col_a, col_b, row_e, row_o), 1 << 20)
    diag_e = send(pair_e, diag_e)
    diag_o = send(pair_o, diag_o)
    lap_fwd, lap_adj = kernel(
        laplace_kernel, "vvvv", (flat,) * 2, (flat_fwd, flat_adj) + inner, 2 << 30, 8, parts)
    speed2, mid_fwd, mid_adj, up, down = kernel(
        advance_kernel, "s" + "v" * 16, (shape(AX, depth, Y), flat, flat, rim_shape, rim_shape),
        (flags, tagged, col_a, col_b, row_e, row_o, diag_e, diag_o, lap_fwd, lap_adj, flat_fwd, flat_adj, fwd_in1, adj_in1,
         below.reshape(AX * 8, Y), above.reshape(AX * 8, Y)) + rim, 1 << 30, 8, both)
    below = send(to_up, up, "slab")
    above = send(to_down, down, "slab")
    lap_fwd, lap_adj = kernel(laplace_kernel, "vvvv", (flat,) * 2, (mid_fwd, mid_adj) + inner, 2 << 30, 8, parts)
    fwd_in2, adj_in2 = kernel(inject_again_kernel, "vvvv", (flat, flat), tuple(points), 2 << 30, 12, hot)
    own, col, row, diag = kernel(
        image_kernel, "s" + "v" * 12, (piece,) * 4,
        (flags, speed2.reshape(FLAT, Y), lap_fwd, lap_adj, flat_fwd, flat_adj, mid_fwd, mid_adj, fwd_in2, adj_in2,
         below.reshape(AX * 8, Y), above.reshape(AX * 8, Y)) + rim, 1 << 30, 8, [pltpu.VMEM((AX, depth, Y), F32)] + both)
    back_e = send(pair_e, diag)
    back_o = send(pair_o, diag)
    sum_a, sum_b = kernel(
        bucket_kernel, "svvvvv", (piece,) * 2, (flags, col, back_e, back_o, tag_e, tag_o), 1 << 20)
    sum_b = send(pair_b, sum_b)
    sum_a = send(pair_a, sum_a)
    same_e = send(pair_e, row)
    same_o = send(pair_o, row)
    near, twice = kernel(
        near_kernel, "s" + "v" * 7, (piece, piece), (flags, tagged, own, same_e, same_o, tag_e, tag_o, sum_a), 1 << 20)
    return (near + twice * sum_b)[None]


def solution(mesh):
    placed = (
        P("shot", None, "slab", None),
        P("shot", None, "slab", None),
        P("shot", None, "slab", None),
        P("shot", None),
        P("shot", None),
        P("shot", None, None),
        P("shot"),
        P("shot", None),
        P("shot", None, None),
    )
    return jax.shard_map(steps, mesh=mesh, in_specs=placed, out_specs=P("shot", None, "slab", None), check_vma=False)
```

```python
import functools

import jax
import jax.numpy as jnp
import numpy as np
from jax import lax
from jax.experimental import pallas as pl
from jax.experimental.pallas import tpu as pltpu
from jax.sharding import PartitionSpec as P


TILES_Y = 4
SCALE = 5040.0
STENCIL = (8064.0, -1008.0, 128.0, -9.0)
CENTRE_XZ = -43008.0
CENTRE_Y = -42.0

BX = 8
Z = 16
Y = 256
Y_BITS = 8
AX = 64
ROWS = BX * Z
BLOCKS = AX // BX
HOT = 512
FLAT = AX * Z
F32 = jnp.float32
BF16 = jnp.bfloat16
VMEM = pl.BlockSpec(memory_space=pltpu.VMEM)
SMEM = pl.BlockSpec(memory_space=pltpu.SMEM)
HBM = pl.BlockSpec(memory_space=pltpu.HBM)
PIECES = 4


def weight(distance):
    distance = np.abs(distance)
    table = np.array((0.0,) + STENCIL + (0.0,))
    return table[np.minimum(distance, 5)]


def exact(matrix):
    narrow = matrix.astype(np.float32).astype(jnp.bfloat16)
    assert np.array_equal(narrow.astype(np.float64), matrix)
    return jnp.asarray(narrow)


def along_xz():
    out_x, out_z = np.divmod(np.arange(ROWS), Z)
    in_x, in_z = np.divmod(np.arange(2 * ROWS), Z)
    kinds = []
    for lead in (0, 4, 8):
        dx = out_x[:, None] - (in_x[None, :] - lead)
        dz = out_z[:, None] - in_z[None, :]
        both = np.where(dz == 0, weight(dx), 0.0) + np.where(dx == 0, weight(dz), 0.0)
        kinds.append(both + np.where((dx == 0) & (dz == 0), CENTRE_XZ, 0.0))
    return np.stack(kinds)


def along_y():
    at = np.arange(Y)
    return weight(at[:, None] - at[None, :]) + CENTRE_Y * np.eye(Y)


def along_halo():
    field, rest = np.divmod(np.arange(ROWS), BX * 8)
    out_x, out_s = np.divmod(rest, 8)
    out_z = np.where(out_s < 4, out_s, Z - 8 + out_s)
    side, rest = np.divmod(np.arange(ROWS), BX * 8)
    in_x, in_s = np.divmod(rest, 8)
    in_z = np.where(side == 0, in_s % 4 - 4, Z + in_s % 4)
    same = (out_x[:, None] == in_x[None, :]) & (field[:, None] == in_s[None, :] // 4)
    return np.where(same, weight(out_z[:, None] - in_z[None, :]), 0.0)


def dot(a, b):
    return jnp.dot(a, b, preferred_element_type=F32)


def split3(value):
    high = value.astype(BF16)
    rest = value - high.astype(F32)
    middle = rest.astype(BF16)
    return high, middle, (rest - middle.astype(F32)).astype(BF16)


def cost(flops, nbytes):
    return pl.CostEstimate(flops=flops, transcendentals=0, bytes_accessed=nbytes)


def rims(fwd, adj):
    front = lax.broadcasted_iota(jnp.int32, (BX, 8, Y), 1) < 4
    top = jnp.where(front, pltpu.roll(fwd[:, 8:, :], 4, 1), adj[:, 8:, :])
    bottom = jnp.where(front, fwd[:, :8, :], pltpu.roll(adj[:, :8, :], 4, 1))
    return top, bottom


def load_kernel(anchor_hbm, vel_hbm, fwd_hbm, adj_hbm, tagged, fwd, adj, up, down, flags, anchor, sems):
    anchor_copy = pltpu.make_async_copy(anchor_hbm, anchor, sems.at[2 * PIECES + 1])
    anchor_copy.start()
    rows = vel_hbm.shape[0]
    tile_copy = pltpu.make_async_copy(vel_hbm, tagged.at[pl.ds(0, rows)], sems.at[2 * PIECES])
    size = AX // PIECES
    copies = []
    for n, (source, target) in enumerate(((fwd_hbm, fwd), (adj_hbm, adj))):
        for i in range(PIECES):
            at = pl.ds(i * size, size)
            copies.append(pltpu.make_async_copy(source.at[at], target.at[at], sems.at[n * PIECES + i]))
    for copy in copies:
        copy.start()
    tile_copy.start()
    anchor_copy.wait()
    device = lax.axis_index("shot")
    home_row = device // TILES_Y
    home_col = device - home_row * TILES_Y
    part_row = home_row - anchor[0, 0]
    part_col = home_col - anchor[0, 1]
    side_row = 1 - 2 * part_row
    side_col = 1 - 2 * part_col
    toward_e = 1 - 2 * (home_row & 1)
    toward_a = 1 - 2 * (home_col & 1)
    flags[0] = part_row
    flags[1] = part_col
    flags[2] = jnp.where(side_row == toward_e, 1, 0)
    flags[3] = jnp.where(side_col == toward_a, 1, 0)
    flags[4] = toward_e
    flags[5] = toward_a
    tagged[rows] = jnp.full(tagged.shape[1:], side_row.astype(F32))
    tagged[rows + 1] = jnp.full(tagged.shape[1:], side_col.astype(F32))

    for copy in copies:
        copy.wait()

    def step(b, _):
        at = pl.ds(b * BX, BX)
        up[at], down[at] = rims(fwd[at], adj[at])
        return 0

    lax.fori_loop(0, BLOCKS, step, 0)
    tile_copy.wait()


def inner_laplace(b, parts, xz, y, result):
    pair = pl.ds(pl.multiple_of(b * 2 * ROWS, 2 * ROWS), 2 * ROWS)
    high, middle, low = parts
    total = dot(low[pair], y[...]) + dot(middle[pair], y[...]) + dot(high[pair], y[...])
    for i in range(2):
        block = 2 * b + i
        kind = jnp.where(block == 0, 0, jnp.where(block == BLOCKS - 1, 2, 1))
        first = jnp.clip(block * BX - 4, 0, AX - 2 * BX) * Z
        window = pl.ds(pl.multiple_of(first, 64), 2 * ROWS)
        part = dot(xz[kind], low[window]) + dot(xz[kind], middle[window]) + dot(xz[kind], high[window])
        result[pl.ds(pl.multiple_of(block * ROWS, ROWS), ROWS)] = part + total[i * ROWS : (i + 1) * ROWS]


def split_all(field, parts):
    def step(b, _):
        at = pl.ds(pl.multiple_of(b * ROWS, ROWS), ROWS)
        parts[0][at], parts[1][at], parts[2][at] = split3(field[at])
        return 0

    lax.fori_loop(0, BLOCKS, step, 0)


def table_of(cells, amounts, first_layer, total_depth, table):
    count = cells.shape[1]
    column = cells >> Y_BITS
    cell_x = ((column.astype(F32) + 0.5) * (1.0 / total_depth)).astype(jnp.int32)
    cell_z = column - cell_x * total_depth - first_layer
    inside = (cell_z >= 0) & (cell_z < Z)
    table[...] = jnp.full(table.shape, -1.0, F32)
    table[0:1, 0:count] = jnp.where(inside, cell_x * Z + cell_z, -1).astype(F32)
    table[1:2, 0:count] = (cells & (Y - 1)).astype(F32)
    table[2:3, 0:count] = amounts[0]
    table[3:4, 0:count] = amounts[1]


def ones_of(points, ones):
    def step(i, _):
        at = pl.ds(pl.multiple_of(i * 128, 128), 128)
        place = jnp.broadcast_to(points[1:2, at], (128, 128)).T
        y = lax.broadcasted_iota(jnp.int32, (128, 128), 1).astype(F32)
        for n in range(Y // 128):
            ones[at, pl.ds(n * 128, 128)] = jnp.where(place == y + float(n * 128), 1.0, 0.0).astype(BF16)
        return 0

    lax.fori_loop(0, points.shape[1] // 128, step, 0)


def hot_rows(b, points, n, hot):
    count = points.shape[1]
    amount = points[2 + n : 3 + n, :]
    part = amount.astype(BF16).astype(F32)
    rest = (amount - part).astype(BF16).astype(F32)
    rows = points[0:1, :].astype(jnp.int32)
    for i in range(HOT // 128):
        hit = lax.broadcasted_iota(jnp.int32, (128, count), 0) + (b * HOT + i * 128) == rows
        hot[pl.ds(i * 128, 128)] = jnp.where(hit, part, 0.0).astype(BF16)
        hot[pl.ds(HOT + i * 128, 128)] = jnp.where(hit, rest, 0.0).astype(BF16)


def inject_all(n, shots, receivers, shot_ones, receiver_ones, fwd_in, adj_in, shot_hot, hot):
    def step(b, _):
        at = pl.ds(pl.multiple_of(b * HOT, HOT), HOT)
        for points, ones, rows, field in ((shots, shot_ones, shot_hot, fwd_in), (receivers, receiver_ones, hot, adj_in)):
            hot_rows(b, points, n, rows)
            both = dot(rows[...], ones[...])
            field[at] = both[:HOT] + both[HOT:]
        return 0

    lax.fori_loop(0, FLAT // HOT, step, 0)


def inject_kernel(total_depth, shot_count, source_cell, wavelet, receiver_cell, residual,
                  fwd_in, adj_in, shots, receivers, shot_ones, receiver_ones, *hot):
    first_layer = lax.axis_index("slab") * Z
    active = lax.broadcasted_iota(jnp.int32, source_cell.shape, 1) < shot_count[0]
    waves = [jnp.where(active, wavelet[i : i + 1, :], 0.0) for i in range(2)]
    table_of(source_cell[...], waves, first_layer, total_depth, shots)
    table_of(receiver_cell[...], [residual[1:2, :], residual[0:1, :]], first_layer, total_depth, receivers)
    ones_of(shots, shot_ones)
    ones_of(receivers, receiver_ones)
    inject_all(0, shots, receivers, shot_ones, receiver_ones, fwd_in, adj_in, *hot)


def inject_again_kernel(shots, receivers, shot_ones, receiver_ones, fwd_in, adj_in, *hot):
    inject_all(1, shots, receivers, shot_ones, receiver_ones, fwd_in, adj_in, *hot)


def laplace_kernel(fwd, adj, xz, y, lap_fwd, lap_adj, f0, f1, f2, a0, a1, a2):
    split_all(fwd, (f0, f1, f2))
    split_all(adj, (a0, a1, a2))

    def step(b, _):
        inner_laplace(b, (f0, f1, f2), xz, y, lap_fwd)
        inner_laplace(b, (a0, a1, a2), xz, y, lap_adj)
        return 0

    lax.fori_loop(0, BLOCKS // 2, step, 0)


def halo_part(b, below, above, halo, both):
    at = pl.ds(pl.multiple_of(b * (ROWS // 2), ROWS // 2), ROWS // 2)
    high, middle, low = split3(jnp.concatenate([below[at], above[at]], 0))
    both[...] = dot(halo[...], low) + dot(halo[...], middle) + dot(halo[...], high)


def halo_of(i, both):
    front = lax.broadcasted_iota(jnp.int32, (8, Y), 0) < 4
    fields = []
    for field in (0, 1):
        part = both[pl.ds(field * (ROWS // 2) + i * 8, 8)]
        fields.append(jnp.concatenate([jnp.where(front, part, 0.0), jnp.where(front, 0.0, part)], 0))
    return fields


def advance_kernel(flags, own, col_a, col_b, row_e, row_o, diag_e, diag_o, lap_fwd, lap_adj, fwd, adj, fwd_in, adj_in,
                   below, above, halo, speed2, mid_fwd, mid_adj, up, down, both):
    half = col_b.shape[0]
    wide = own.shape[2]
    with_e = flags[2] == 1
    with_a = flags[3] == 1
    row_at = flags[0] * half
    row_to = (1 - flags[0]) * half
    col_at = pl.ds(pl.multiple_of(flags[1] * wide, wide), wide)
    col_to = pl.ds(pl.multiple_of((1 - flags[1]) * wide, wide), wide)

    def assemble(i, _):
        at = pl.ds(i * 8, 8)
        near = pl.ds(row_at + i * 8, 8)
        far = pl.ds(row_to + i * 8, 8)
        speed = own[at]
        speed2[near, :, col_at] = speed * speed * (1.0 / SCALE)
        speed = jnp.where(with_a, col_a[at], col_b[at])
        speed2[near, :, col_to] = speed * speed * (1.0 / SCALE)
        speed = jnp.where(with_e, row_e[at], row_o[at])
        speed2[far, :, col_at] = speed * speed * (1.0 / SCALE)
        speed = jnp.where(with_e, diag_e[at], diag_o[at])
        speed2[far, :, col_to] = speed * speed * (1.0 / SCALE)
        return 0

    lax.fori_loop(0, half // 8, assemble, 0)

    def step(b, _):
        halo_part(b, below, above, halo, both)
        front = lax.broadcasted_iota(jnp.int32, (8, Y), 0) < 4
        for i in range(BX):
            x = b * BX + i
            at = pl.ds(pl.multiple_of(x * Z, Z), Z)
            halo_fwd, halo_adj = halo_of(i, both)
            c = speed2[x]
            new_fwd = fwd[at] + (c * (lap_fwd[at] + halo_fwd) + fwd_in[at])
            new_adj = adj[at] + (c * (lap_adj[at] + halo_adj) + adj_in[at])
            mid_fwd[at] = new_fwd
            mid_adj[at] = new_adj
            up[x] = jnp.where(front, pltpu.roll(new_fwd[8:], 4, 0), new_adj[8:])
            down[x] = jnp.where(front, new_fwd[:8], pltpu.roll(new_adj[:8], 4, 0))
        return 0

    lax.fori_loop(0, BLOCKS, step, 0)


def image_kernel(flags, speed2, lap_fwd, lap_adj, fwd, adj, mid_fwd, mid_adj, fwd_in, adj_in, below, above, halo,
                 own, col, row, diag, image, both):
    def step(b, _):
        halo_part(b, below, above, halo, both)
        for i in range(BX):
            x = b * BX + i
            at = pl.ds(pl.multiple_of(x * Z, Z), Z)
            halo_fwd, halo_adj = halo_of(i, both)
            c = speed2[at]
            second_fwd = c * (lap_fwd[at] + halo_fwd) + fwd_in[at]
            second_adj = c * (lap_adj[at] + halo_adj) + adj_in[at]
            later = mid_adj[at]
            earlier = 2.0 * later - adj[at] + second_adj
            image[x] = earlier * (mid_fwd[at] - fwd[at]) + later * second_fwd
        return 0

    lax.fori_loop(0, BLOCKS, step, 0)
    half = own.shape[0]
    wide = own.shape[2]
    row_at = flags[0] * half
    row_to = (1 - flags[0]) * half
    col_at = pl.ds(pl.multiple_of(flags[1] * wide, wide), wide)
    col_to = pl.ds(pl.multiple_of((1 - flags[1]) * wide, wide), wide)

    def hand_out(i, _):
        at = pl.ds(i * 8, 8)
        near = pl.ds(row_at + i * 8, 8)
        far = pl.ds(row_to + i * 8, 8)
        own[at] = image[near, :, col_at]
        col[at] = image[near, :, col_to]
        row[at] = image[far, :, col_at]
        diag[at] = image[far, :, col_to]
        return 0

    lax.fori_loop(0, half // 8, hand_out, 0)


def swaps(count):
    rows = count // TILES_Y
    a = [(s, s ^ 1) for s in range(count)]
    b = [(s, s + 1) if s % TILES_Y == 1 else (s, s - 1) for s in range(count) if s % TILES_Y in (1, 2)]
    e = [(s, s + TILES_Y if (s // TILES_Y) % 2 == 0 else s - TILES_Y) for s in range(count)]
    o = []
    for s in range(count):
        other = s // TILES_Y + (1 if (s // TILES_Y) % 2 else -1)
        if 0 <= other < rows:
            o.append((s, other * TILES_Y + s % TILES_Y))
    return a, b, e, o


def select_kernel(flags, col_a, col_b, row_e, row_o, diag_e, diag_o, tag_e, tag_o):
    half = col_b.shape[0]
    toward_a = flags[5].astype(F32)
    tag_e[...] = row_e[half:]
    tag_o[...] = row_o[half:]
    e_wants_a = row_e[half + 1] == toward_a
    o_wants_a = row_o[half + 1] == toward_a

    def step(i, _):
        at = pl.ds(i * 8, 8)
        a = col_a[at]
        b = col_b[at]
        diag_e[at] = jnp.where(e_wants_a[None], a, b)
        diag_o[at] = jnp.where(o_wants_a[None], a, b)
        return 0

    lax.fori_loop(0, half // 8, step, 0)


def bucket_kernel(flags, col, back_e, back_o, tag_e, tag_o, sum_a, sum_b):
    toward_e = flags[4].astype(F32)
    toward_a = flags[5].astype(F32)
    with_a = flags[3] == 1
    from_e = tag_e[0] == -toward_e
    from_o = tag_o[0] == toward_e
    e_a = from_e & (tag_e[1] == toward_a)
    e_b = from_e & (tag_e[1] == -toward_a)
    o_a = from_o & (tag_o[1] == toward_a)
    o_b = from_o & (tag_o[1] == -toward_a)

    def step(i, _):
        at = pl.ds(i * 8, 8)
        c = col[at]
        e = back_e[at]
        o = back_o[at]
        sum_a[at] = jnp.where(with_a, c, 0.0) + jnp.where(e_a[None], e, 0.0) + jnp.where(o_a[None], o, 0.0)
        sum_b[at] = jnp.where(with_a, 0.0, c) + jnp.where(e_b[None], e, 0.0) + jnp.where(o_b[None], o, 0.0)
        return 0

    lax.fori_loop(0, col.shape[0] // 8, step, 0)


def near_kernel(flags, tile, own, same_e, same_o, tag_e, tag_o, sum_a, near, twice):
    toward_e = flags[4].astype(F32)
    from_e = tag_e[0] == -toward_e
    from_o = tag_o[0] == toward_e

    def step(i, _):
        at = pl.ds(i * 8, 8)
        total = own[at] + jnp.where(from_e[None], same_e[at], 0.0) + jnp.where(from_o[None], same_o[at], 0.0)
        double = 2.0 * tile[at]
        twice[at] = double
        near[at] = double * (total + sum_a[at])
        return 0

    lax.fori_loop(0, own.shape[0] // 8, step, 0)


def steps(velocity, fwd_field, adj_field, aperture_anchor, source_cell, wavelet, shot_count, receiver_cell, residual):
    tile = velocity[0]
    half, depth, wide = tile.shape
    slabs = lax.axis_size("slab")
    pair_a, pair_b, pair_e, pair_o = swaps(lax.axis_size("shot"))
    to_up = [(i, i + 1) for i in range(slabs - 1)]
    to_down = [(i + 1, i) for i in range(slabs - 1)]

    def shape(*dims, dtype=F32):
        return jax.ShapeDtypeStruct(dims, dtype)

    def send(pairs, value, axis="shot"):
        return lax.ppermute(value, axis, pairs)

    def kernel(function, ins, outs, args, flops, mib=8, scratch=()):
        places = [{"s": SMEM, "h": HBM, "v": VMEM}[i] for i in ins]
        sent = tuple(SMEM if o.dtype == jnp.int32 else VMEM for o in outs)
        nbytes = sum(int(np.prod(a.shape)) * 4 for a in tuple(args) + tuple(outs))
        return pl.pallas_call(
            function,
            out_shape=tuple(outs),
            in_specs=places,
            out_specs=sent,
            scratch_shapes=list(scratch),
            compiler_params=pltpu.CompilerParams(vmem_limit_bytes=mib * 1024 * 1024),
            cost_estimate=cost(flops, nbytes),
        )(*args)

    piece = shape(half, depth, wide)
    rim_shape = shape(AX, 8, Y)
    flat = shape(FLAT, Y)
    parts = [pltpu.VMEM((FLAT, Y), BF16)] * 6
    both = [pltpu.VMEM((ROWS, Y), F32)]
    inner = (exact(along_xz()), exact(along_y()))
    rim = (exact(along_halo()),)

    col_b = send(pair_b, tile)
    field = shape(AX, depth, Y)
    tagged, fwd, adj, up, down, flags = kernel(
        load_kernel, "hhhh",
        (shape(half + 2, depth, wide), field, field, rim_shape, rim_shape, shape(8, dtype=jnp.int32)),
        tuple(pltpu.with_memory_space_constraint(v, pltpu.HBM) for v in (aperture_anchor, tile, fwd_field[0], adj_field[0])), 1 << 20, 8, [pltpu.SMEM((1, 2), jnp.int32), pltpu.SemaphoreType.DMA((2 * PIECES + 2,))])
    flat_fwd = fwd.reshape(FLAT, Y)
    flat_adj = adj.reshape(FLAT, Y)
    col_a = send(pair_a, tagged)
    row_e = send(pair_e, tagged)
    row_o = send(pair_o, tagged)
    below = send(to_up, up, "slab")
    above = send(to_down, down, "slab")
    recv = receiver_cell.shape[1]

    hot = [pltpu.VMEM((2 * HOT, n), BF16) for n in (128, recv)]
    ones = (shape(128, Y, dtype=BF16), shape(recv, Y, dtype=BF16))
    fwd_in1, adj_in1, *points = kernel(
        functools.partial(inject_kernel, depth * slabs), "svvvv",
        (flat, flat, shape(8, 128), shape(8, recv)) + ones,
        (shot_count, source_cell, wavelet[0], receiver_cell, residual[0]), 2 << 30, 12, hot)
    diag_e, diag_o, tag_e, tag_o = kernel(
        select_kernel, "svvvv", (piece, piece, shape(2, depth, wide), shape(2, depth, wide)),
        (flags, col_a, col_b, row_e, row_o), 1 << 20)
    diag_e = send(pair_e, diag_e)
    diag_o = send(pair_o, diag_o)
    lap_fwd, lap_adj = kernel(
        laplace_kernel, "vvvv", (flat,) * 2, (flat_fwd, flat_adj) + inner, 2 << 30, 8, parts)
    speed2, mid_fwd, mid_adj, up, down = kernel(
        advance_kernel, "s" + "v" * 16, (shape(AX, depth, Y), flat, flat, rim_shape, rim_shape),
        (flags, tagged, col_a, col_b, row_e, row_o, diag_e, diag_o, lap_fwd, lap_adj, flat_fwd, flat_adj, fwd_in1, adj_in1,
         below.reshape(AX * 8, Y), above.reshape(AX * 8, Y)) + rim, 1 << 30, 8, both)
    below = send(to_up, up, "slab")
    above = send(to_down, down, "slab")
    lap_fwd, lap_adj = kernel(laplace_kernel, "vvvv", (flat,) * 2, (mid_fwd, mid_adj) + inner, 2 << 30, 8, parts)
    fwd_in2, adj_in2 = kernel(inject_again_kernel, "vvvv", (flat, flat), tuple(points), 2 << 30, 12, hot)
    own, col, row, diag = kernel(
        image_kernel, "s" + "v" * 12, (piece,) * 4,
        (flags, speed2.reshape(FLAT, Y), lap_fwd, lap_adj, flat_fwd, flat_adj, mid_fwd, mid_adj, fwd_in2, adj_in2,
         below.reshape(AX * 8, Y), above.reshape(AX * 8, Y)) + rim, 1 << 30, 8, [pltpu.VMEM((AX, depth, Y), F32)] + both)
    back_e = send(pair_e, diag)
    back_o = send(pair_o, diag)
    sum_a, sum_b = kernel(
        bucket_kernel, "svvvvv", (piece,) * 2, (flags, col, back_e, back_o, tag_e, tag_o), 1 << 20)
    sum_b = send(pair_b, sum_b)
    sum_a = send(pair_a, sum_a)
    same_e = send(pair_e, row)
    same_o = send(pair_o, row)
    near, twice = kernel(
        near_kernel, "s" + "v" * 7, (piece, piece), (flags, tagged, own, same_e, same_o, tag_e, tag_o, sum_a), 1 << 20)
    return (near + twice * sum_b)[None]


def solution(mesh):
    placed = (
        P("shot", None, "slab", None),
        P("shot", None, "slab", None),
        P("shot", None, "slab", None),
        P("shot", None),
        P("shot", None),
        P("shot", None, None),
        P("shot"),
        P("shot", None),
        P("shot", None, None),
    )
    return jax.shard_map(steps, mesh=mesh, in_specs=placed, out_specs=P("shot", None, "slab", None), check_vma=False)
```

```python
import functools

import jax
import jax.numpy as jnp
import numpy as np
from jax import lax
from jax.experimental import pallas as pl
from jax.experimental.pallas import tpu as pltpu
from jax.sharding import PartitionSpec as P


TILES_Y = 4
SCALE = 5040.0
STENCIL = (8064.0, -1008.0, 128.0, -9.0)
CENTRE_XZ = -43008.0
CENTRE_Y = -42.0

BX = 8
Z = 16
Y = 256
Y_BITS = 8
AX = 64
ROWS = BX * Z
BLOCKS = AX // BX
HOT = 512
FLAT = AX * Z
F32 = jnp.float32
BF16 = jnp.bfloat16
VMEM = pl.BlockSpec(memory_space=pltpu.VMEM)
SMEM = pl.BlockSpec(memory_space=pltpu.SMEM)
HBM = pl.BlockSpec(memory_space=pltpu.HBM)
PIECES = 4


def weight(distance):
    distance = np.abs(distance)
    table = np.array((0.0,) + STENCIL + (0.0,))
    return table[np.minimum(distance, 5)]


def exact(matrix):
    narrow = matrix.astype(np.float32).astype(jnp.bfloat16)
    assert np.array_equal(narrow.astype(np.float64), matrix)
    return jnp.asarray(narrow)


def along_xz():
    out_x, out_z = np.divmod(np.arange(ROWS), Z)
    in_x, in_z = np.divmod(np.arange(2 * ROWS), Z)
    kinds = []
    for lead in (0, 4, 8):
        dx = out_x[:, None] - (in_x[None, :] - lead)
        dz = out_z[:, None] - in_z[None, :]
        both = np.where(dz == 0, weight(dx), 0.0) + np.where(dx == 0, weight(dz), 0.0)
        kinds.append(both + np.where((dx == 0) & (dz == 0), CENTRE_XZ, 0.0))
    return np.stack(kinds)


def along_y():
    at = np.arange(Y)
    return weight(at[:, None] - at[None, :]) + CENTRE_Y * np.eye(Y)


def along_halo():
    field, rest = np.divmod(np.arange(ROWS), BX * 8)
    out_x, out_s = np.divmod(rest, 8)
    out_z = np.where(out_s < 4, out_s, Z - 8 + out_s)
    side, rest = np.divmod(np.arange(ROWS), BX * 8)
    in_x, in_s = np.divmod(rest, 8)
    in_z = np.where(side == 0, in_s % 4 - 4, Z + in_s % 4)
    same = (out_x[:, None] == in_x[None, :]) & (field[:, None] == in_s[None, :] // 4)
    return np.where(same, weight(out_z[:, None] - in_z[None, :]), 0.0)


def dot(a, b):
    return jnp.dot(a, b, preferred_element_type=F32)


def split3(value):
    high = value.astype(BF16)
    rest = value - high.astype(F32)
    middle = rest.astype(BF16)
    return high, middle, (rest - middle.astype(F32)).astype(BF16)


def cost(flops, nbytes):
    return pl.CostEstimate(flops=flops, transcendentals=0, bytes_accessed=nbytes)


def rims(fwd, adj):
    front = lax.broadcasted_iota(jnp.int32, (BX, 8, Y), 1) < 4
    top = jnp.where(front, pltpu.roll(fwd[:, 8:, :], 4, 1), adj[:, 8:, :])
    bottom = jnp.where(front, fwd[:, :8, :], pltpu.roll(adj[:, :8, :], 4, 1))
    return top, bottom


def load_kernel(anchor_hbm, vel_hbm, fwd_hbm, adj_hbm, tagged, fwd, adj, up, down, flags, anchor, sems):
    anchor_copy = pltpu.make_async_copy(anchor_hbm, anchor, sems.at[2 * PIECES + 1])
    anchor_copy.start()
    rows = vel_hbm.shape[0]
    tile_copy = pltpu.make_async_copy(vel_hbm, tagged.at[pl.ds(0, rows)], sems.at[2 * PIECES])
    size = AX // PIECES
    copies = []
    for n, (source, target) in enumerate(((fwd_hbm, fwd), (adj_hbm, adj))):
        for i in range(PIECES):
            at = pl.ds(i * size, size)
            copies.append(pltpu.make_async_copy(source.at[at], target.at[at], sems.at[n * PIECES + i]))
    for copy in copies:
        copy.start()
    tile_copy.start()
    anchor_copy.wait()
    device = lax.axis_index("shot")
    home_row = device // TILES_Y
    home_col = device - home_row * TILES_Y
    part_row = home_row - anchor[0, 0]
    part_col = home_col - anchor[0, 1]
    side_row = 1 - 2 * part_row
    side_col = 1 - 2 * part_col
    toward_e = 1 - 2 * (home_row & 1)
    toward_a = 1 - 2 * (home_col & 1)
    flags[0] = part_row
    flags[1] = part_col
    flags[2] = jnp.where(side_row == toward_e, 1, 0)
    flags[3] = jnp.where(side_col == toward_a, 1, 0)
    flags[4] = toward_e
    flags[5] = toward_a
    tagged[rows] = jnp.full(tagged.shape[1:], side_row.astype(F32))
    tagged[rows + 1] = jnp.full(tagged.shape[1:], side_col.astype(F32))

    for copy in copies:
        copy.wait()

    def step(b, _):
        at = pl.ds(b * BX, BX)
        up[at], down[at] = rims(fwd[at], adj[at])
        return 0

    lax.fori_loop(0, BLOCKS, step, 0)
    tile_copy.wait()


def inner_laplace(b, parts, xz, y, result):
    pair = pl.ds(pl.multiple_of(b * 2 * ROWS, 2 * ROWS), 2 * ROWS)
    high, middle, low = parts
    total = dot(low[pair], y[...]) + dot(middle[pair], y[...]) + dot(high[pair], y[...])
    for i in range(2):
        block = 2 * b + i
        kind = jnp.where(block == 0, 0, jnp.where(block == BLOCKS - 1, 2, 1))
        first = jnp.clip(block * BX - 4, 0, AX - 2 * BX) * Z
        window = pl.ds(pl.multiple_of(first, 64), 2 * ROWS)
        part = dot(xz[kind], low[window]) + dot(xz[kind], middle[window]) + dot(xz[kind], high[window])
        result[pl.ds(pl.multiple_of(block * ROWS, ROWS), ROWS)] = part + total[i * ROWS : (i + 1) * ROWS]


def split_all(field, parts):
    def step(b, _):
        at = pl.ds(pl.multiple_of(b * ROWS, ROWS), ROWS)
        parts[0][at], parts[1][at], parts[2][at] = split3(field[at])
        return 0

    lax.fori_loop(0, BLOCKS, step, 0)


def table_of(cells, amounts, first_layer, total_depth, table):
    count = cells.shape[1]
    column = cells >> Y_BITS
    cell_x = ((column.astype(F32) + 0.5) * (1.0 / total_depth)).astype(jnp.int32)
    cell_z = column - cell_x * total_depth - first_layer
    inside = (cell_z >= 0) & (cell_z < Z)
    table[...] = jnp.full(table.shape, -1.0, F32)
    table[0:1, 0:count] = jnp.where(inside, cell_x * Z + cell_z, -1).astype(F32)
    table[1:2, 0:count] = (cells & (Y - 1)).astype(F32)
    table[2:3, 0:count] = amounts[0]
    table[3:4, 0:count] = amounts[1]


def ones_of(points, ones):
    def step(i, _):
        at = pl.ds(pl.multiple_of(i * 128, 128), 128)
        place = jnp.broadcast_to(points[1:2, at], (128, 128)).T
        y = lax.broadcasted_iota(jnp.int32, (128, 128), 1).astype(F32)
        for n in range(Y // 128):
            ones[at, pl.ds(n * 128, 128)] = jnp.where(place == y + float(n * 128), 1.0, 0.0).astype(BF16)
        return 0

    lax.fori_loop(0, points.shape[1] // 128, step, 0)


def hot_rows(b, points, n, hot):
    count = points.shape[1]
    amount = points[2 + n : 3 + n, :]
    part = amount.astype(BF16).astype(F32)
    rest = (amount - part).astype(BF16).astype(F32)
    rows = points[0:1, :].astype(jnp.int32)
    for i in range(HOT // 128):
        hit = lax.broadcasted_iota(jnp.int32, (128, count), 0) + (b * HOT + i * 128) == rows
        hot[pl.ds(i * 128, 128)] = jnp.where(hit, part, 0.0).astype(BF16)
        hot[pl.ds(HOT + i * 128, 128)] = jnp.where(hit, rest, 0.0).astype(BF16)


def inject_all(n, shots, receivers, shot_ones, receiver_ones, fwd_in, adj_in, shot_hot, hot):
    def step(b, _):
        at = pl.ds(pl.multiple_of(b * HOT, HOT), HOT)
        for points, ones, rows, field in ((shots, shot_ones, shot_hot, fwd_in), (receivers, receiver_ones, hot, adj_in)):
            hot_rows(b, points, n, rows)
            both = dot(rows[...], ones[...])
            field[at] = both[:HOT] + both[HOT:]
        return 0

    lax.fori_loop(0, FLAT // HOT, step, 0)


def inject_kernel(total_depth, shot_count, source_cell, wavelet, receiver_cell, residual,
                  fwd_in, adj_in, shots, receivers, shot_ones, receiver_ones, *hot):
    first_layer = lax.axis_index("slab") * Z
    active = lax.broadcasted_iota(jnp.int32, source_cell.shape, 1) < shot_count[0]
    waves = [jnp.where(active, wavelet[i : i + 1, :], 0.0) for i in range(2)]
    table_of(source_cell[...], waves, first_layer, total_depth, shots)
    table_of(receiver_cell[...], [residual[1:2, :], residual[0:1, :]], first_layer, total_depth, receivers)
    ones_of(shots, shot_ones)
    ones_of(receivers, receiver_ones)
    inject_all(0, shots, receivers, shot_ones, receiver_ones, fwd_in, adj_in, *hot)


def inject_again_kernel(shots, receivers, shot_ones, receiver_ones, fwd_in, adj_in, *hot):
    inject_all(1, shots, receivers, shot_ones, receiver_ones, fwd_in, adj_in, *hot)


def laplace_kernel(fwd, adj, xz, y, lap_fwd, lap_adj, f0, f1, f2, a0, a1, a2):
    split_all(fwd, (f0, f1, f2))
    split_all(adj, (a0, a1, a2))

    def step(b, _):
        inner_laplace(b, (f0, f1, f2), xz, y, lap_fwd)
        inner_laplace(b, (a0, a1, a2), xz, y, lap_adj)
        return 0

    lax.fori_loop(0, BLOCKS // 2, step, 0)


def halo_part(b, below, above, halo, both):
    at = pl.ds(pl.multiple_of(b * (ROWS // 2), ROWS // 2), ROWS // 2)
    high, middle, low = split3(jnp.concatenate([below[at], above[at]], 0))
    both[...] = dot(halo[...], low) + dot(halo[...], middle) + dot(halo[...], high)


def halo_of(i, both):
    front = lax.broadcasted_iota(jnp.int32, (8, Y), 0) < 4
    fields = []
    for field in (0, 1):
        part = both[pl.ds(field * (ROWS // 2) + i * 8, 8)]
        fields.append(jnp.concatenate([jnp.where(front, part, 0.0), jnp.where(front, 0.0, part)], 0))
    return fields


def advance_kernel(flags, own, col_a, col_b, row_e, row_o, diag_e, diag_o, lap_fwd, lap_adj, fwd, adj, fwd_in, adj_in,
                   below, above, halo, speed2, mid_fwd, mid_adj, up, down, both):
    half = col_b.shape[0]
    wide = own.shape[2]
    with_e = flags[2] == 1
    with_a = flags[3] == 1
    row_at = flags[0] * half
    row_to = (1 - flags[0]) * half
    col_at = pl.ds(pl.multiple_of(flags[1] * wide, wide), wide)
    col_to = pl.ds(pl.multiple_of((1 - flags[1]) * wide, wide), wide)

    def assemble(i, _):
        at = pl.ds(i * 8, 8)
        near = pl.ds(row_at + i * 8, 8)
        far = pl.ds(row_to + i * 8, 8)
        speed = own[at]
        speed2[near, :, col_at] = speed * speed * (1.0 / SCALE)
        speed = jnp.where(with_a, col_a[at], col_b[at])
        speed2[near, :, col_to] = speed * speed * (1.0 / SCALE)
        speed = jnp.where(with_e, row_e[at], row_o[at])
        speed2[far, :, col_at] = speed * speed * (1.0 / SCALE)
        speed = jnp.where(with_e, diag_e[at], diag_o[at])
        speed2[far, :, col_to] = speed * speed * (1.0 / SCALE)
        return 0

    lax.fori_loop(0, half // 8, assemble, 0)

    def step(b, _):
        halo_part(b, below, above, halo, both)
        front = lax.broadcasted_iota(jnp.int32, (8, Y), 0) < 4
        for i in range(BX):
            x = b * BX + i
            at = pl.ds(pl.multiple_of(x * Z, Z), Z)
            halo_fwd, halo_adj = halo_of(i, both)
            c = speed2[x]
            new_fwd = fwd[at] + (c * (lap_fwd[at] + halo_fwd) + fwd_in[at])
            new_adj = adj[at] + (c * (lap_adj[at] + halo_adj) + adj_in[at])
            mid_fwd[at] = new_fwd
            mid_adj[at] = new_adj
            up[x] = jnp.where(front, pltpu.roll(new_fwd[8:], 4, 0), new_adj[8:])
            down[x] = jnp.where(front, new_fwd[:8], pltpu.roll(new_adj[:8], 4, 0))
        return 0

    lax.fori_loop(0, BLOCKS, step, 0)


def blend_kernel(speed2, lap_fwd, lap_adj, fwd, adj, mid_fwd, mid_adj, fwd_in, adj_in, inner, by_adj, by_fwd):
    def step(b, _):
        at = pl.ds(pl.multiple_of(b * Z * 2, Z * 2), Z * 2)
        c = speed2[at]
        later = mid_adj[at]
        first = mid_fwd[at] - fwd[at]
        second_fwd = c * lap_fwd[at] + fwd_in[at]
        earlier = 2.0 * later - adj[at] + (c * lap_adj[at] + adj_in[at])
        inner[at] = earlier * first + later * second_fwd
        by_adj[at] = c * first
        by_fwd[at] = c * later
        return 0

    lax.fori_loop(0, FLAT // (Z * 2), step, 0, unroll=2)


def image_kernel(flags, inner, by_adj, by_fwd, below, above, halo, own, col, row, diag, image, both):
    def step(b, _):
        halo_part(b, below, above, halo, both)
        for i in range(BX):
            x = b * BX + i
            at = pl.ds(pl.multiple_of(x * Z, Z), Z)
            halo_fwd, halo_adj = halo_of(i, both)
            image[x] = inner[at] + by_adj[at] * halo_adj + by_fwd[at] * halo_fwd
        return 0

    lax.fori_loop(0, BLOCKS, step, 0)
    half = own.shape[0]
    wide = own.shape[2]
    row_at = flags[0] * half
    row_to = (1 - flags[0]) * half
    col_at = pl.ds(pl.multiple_of(flags[1] * wide, wide), wide)
    col_to = pl.ds(pl.multiple_of((1 - flags[1]) * wide, wide), wide)

    def hand_out(i, _):
        at = pl.ds(i * 8, 8)
        near = pl.ds(row_at + i * 8, 8)
        far = pl.ds(row_to + i * 8, 8)
        own[at] = image[near, :, col_at]
        col[at] = image[near, :, col_to]
        row[at] = image[far, :, col_at]
        diag[at] = image[far, :, col_to]
        return 0

    lax.fori_loop(0, half // 8, hand_out, 0)


def swaps(count):
    rows = count // TILES_Y
    a = [(s, s ^ 1) for s in range(count)]
    b = [(s, s + 1) if s % TILES_Y == 1 else (s, s - 1) for s in range(count) if s % TILES_Y in (1, 2)]
    e = [(s, s + TILES_Y if (s // TILES_Y) % 2 == 0 else s - TILES_Y) for s in range(count)]
    o = []
    for s in range(count):
        other = s // TILES_Y + (1 if (s // TILES_Y) % 2 else -1)
        if 0 <= other < rows:
            o.append((s, other * TILES_Y + s % TILES_Y))
    return a, b, e, o


def select_kernel(flags, col_a, col_b, row_e, row_o, diag_e, diag_o, tag_e, tag_o):
    half = col_b.shape[0]
    toward_a = flags[5].astype(F32)
    tag_e[...] = row_e[half:]
    tag_o[...] = row_o[half:]
    e_wants_a = row_e[half + 1] == toward_a
    o_wants_a = row_o[half + 1] == toward_a

    def step(i, _):
        at = pl.ds(i * 8, 8)
        a = col_a[at]
        b = col_b[at]
        diag_e[at] = jnp.where(e_wants_a[None], a, b)
        diag_o[at] = jnp.where(o_wants_a[None], a, b)
        return 0

    lax.fori_loop(0, half // 8, step, 0)


def bucket_kernel(flags, col, back_e, back_o, tag_e, tag_o, sum_a, sum_b):
    toward_e = flags[4].astype(F32)
    toward_a = flags[5].astype(F32)
    with_a = flags[3] == 1
    from_e = tag_e[0] == -toward_e
    from_o = tag_o[0] == toward_e
    e_a = from_e & (tag_e[1] == toward_a)
    e_b = from_e & (tag_e[1] == -toward_a)
    o_a = from_o & (tag_o[1] == toward_a)
    o_b = from_o & (tag_o[1] == -toward_a)

    def step(i, _):
        at = pl.ds(i * 8, 8)
        c = col[at]
        e = back_e[at]
        o = back_o[at]
        sum_a[at] = jnp.where(with_a, c, 0.0) + jnp.where(e_a[None], e, 0.0) + jnp.where(o_a[None], o, 0.0)
        sum_b[at] = jnp.where(with_a, 0.0, c) + jnp.where(e_b[None], e, 0.0) + jnp.where(o_b[None], o, 0.0)
        return 0

    lax.fori_loop(0, col.shape[0] // 8, step, 0)


def near_kernel(flags, tile, own, same_e, same_o, tag_e, tag_o, sum_a, near, twice):
    toward_e = flags[4].astype(F32)
    from_e = tag_e[0] == -toward_e
    from_o = tag_o[0] == toward_e

    def step(i, _):
        at = pl.ds(i * 8, 8)
        total = own[at] + jnp.where(from_e[None], same_e[at], 0.0) + jnp.where(from_o[None], same_o[at], 0.0)
        double = 2.0 * tile[at]
        twice[at] = double
        near[at] = double * (total + sum_a[at])
        return 0

    lax.fori_loop(0, own.shape[0] // 8, step, 0)


def steps(velocity, fwd_field, adj_field, aperture_anchor, source_cell, wavelet, shot_count, receiver_cell, residual):
    tile = velocity[0]
    half, depth, wide = tile.shape
    slabs = lax.axis_size("slab")
    pair_a, pair_b, pair_e, pair_o = swaps(lax.axis_size("shot"))
    to_up = [(i, i + 1) for i in range(slabs - 1)]
    to_down = [(i + 1, i) for i in range(slabs - 1)]

    def shape(*dims, dtype=F32):
        return jax.ShapeDtypeStruct(dims, dtype)

    def send(pairs, value, axis="shot"):
        return lax.ppermute(value, axis, pairs)

    def kernel(function, ins, outs, args, flops, mib=8, scratch=()):
        places = [{"s": SMEM, "h": HBM, "v": VMEM}[i] for i in ins]
        sent = tuple(SMEM if o.dtype == jnp.int32 else VMEM for o in outs)
        nbytes = sum(int(np.prod(a.shape)) * 4 for a in tuple(args) + tuple(outs))
        return pl.pallas_call(
            function,
            out_shape=tuple(outs),
            in_specs=places,
            out_specs=sent,
            scratch_shapes=list(scratch),
            compiler_params=pltpu.CompilerParams(vmem_limit_bytes=mib * 1024 * 1024),
            cost_estimate=cost(flops, nbytes),
        )(*args)

    piece = shape(half, depth, wide)
    rim_shape = shape(AX, 8, Y)
    flat = shape(FLAT, Y)
    parts = [pltpu.VMEM((FLAT, Y), BF16)] * 6
    both = [pltpu.VMEM((ROWS, Y), F32)]
    inner = (exact(along_xz()), exact(along_y()))
    rim = (exact(along_halo()),)

    col_b = send(pair_b, tile)
    field = shape(AX, depth, Y)
    tagged, fwd, adj, up, down, flags = kernel(
        load_kernel, "hhhh",
        (shape(half + 2, depth, wide), field, field, rim_shape, rim_shape, shape(8, dtype=jnp.int32)),
        tuple(pltpu.with_memory_space_constraint(v, pltpu.HBM) for v in (aperture_anchor, tile, fwd_field[0], adj_field[0])), 1 << 20, 8, [pltpu.SMEM((1, 2), jnp.int32), pltpu.SemaphoreType.DMA((2 * PIECES + 2,))])
    flat_fwd = fwd.reshape(FLAT, Y)
    flat_adj = adj.reshape(FLAT, Y)
    col_a = send(pair_a, tagged)
    row_e = send(pair_e, tagged)
    row_o = send(pair_o, tagged)
    below = send(to_up, up, "slab")
    above = send(to_down, down, "slab")
    recv = receiver_cell.shape[1]

    hot = [pltpu.VMEM((2 * HOT, n), BF16) for n in (128, recv)]
    ones = (shape(128, Y, dtype=BF16), shape(recv, Y, dtype=BF16))
    fwd_in1, adj_in1, *points = kernel(
        functools.partial(inject_kernel, depth * slabs), "svvvv",
        (flat, flat, shape(8, 128), shape(8, recv)) + ones,
        (shot_count, source_cell, wavelet[0], receiver_cell, residual[0]), 2 << 30, 12, hot)
    diag_e, diag_o, tag_e, tag_o = kernel(
        select_kernel, "svvvv", (piece, piece, shape(2, depth, wide), shape(2, depth, wide)),
        (flags, col_a, col_b, row_e, row_o), 1 << 20)
    diag_e = send(pair_e, diag_e)
    diag_o = send(pair_o, diag_o)
    lap_fwd, lap_adj = kernel(
        laplace_kernel, "vvvv", (flat,) * 2, (flat_fwd, flat_adj) + inner, 2 << 30, 8, parts)
    speed2, mid_fwd, mid_adj, up, down = kernel(
        advance_kernel, "s" + "v" * 16, (shape(AX, depth, Y), flat, flat, rim_shape, rim_shape),
        (flags, tagged, col_a, col_b, row_e, row_o, diag_e, diag_o, lap_fwd, lap_adj, flat_fwd, flat_adj, fwd_in1, adj_in1,
         below.reshape(AX * 8, Y), above.reshape(AX * 8, Y)) + rim, 1 << 30, 8, both)
    below = send(to_up, up, "slab")
    above = send(to_down, down, "slab")
    lap_fwd, lap_adj = kernel(laplace_kernel, "vvvv", (flat,) * 2, (mid_fwd, mid_adj) + inner, 2 << 30, 8, parts)
    fwd_in2, adj_in2 = kernel(inject_again_kernel, "vvvv", (flat, flat), tuple(points), 2 << 30, 12, hot)
    inner_part, by_adj, by_fwd = kernel(
        blend_kernel, "v" * 9, (flat,) * 3,
        (speed2.reshape(FLAT, Y), lap_fwd, lap_adj, flat_fwd, flat_adj, mid_fwd, mid_adj, fwd_in2, adj_in2), 4 << 20)
    own, col, row, diag = kernel(
        image_kernel, "s" + "v" * 6, (piece,) * 4,
        (flags, inner_part, by_adj, by_fwd, below.reshape(AX * 8, Y), above.reshape(AX * 8, Y)) + rim,
        1 << 30, 8, [pltpu.VMEM((AX, depth, Y), F32)] + both)
    back_e = send(pair_e, diag)
    back_o = send(pair_o, diag)
    sum_a, sum_b = kernel(
        bucket_kernel, "svvvvv", (piece,) * 2, (flags, col, back_e, back_o, tag_e, tag_o), 1 << 20)
    sum_b = send(pair_b, sum_b)
    sum_a = send(pair_a, sum_a)
    same_e = send(pair_e, row)
    same_o = send(pair_o, row)
    near, twice = kernel(
        near_kernel, "s" + "v" * 7, (piece, piece), (flags, tagged, own, same_e, same_o, tag_e, tag_o, sum_a), 1 << 20)
    return (near + twice * sum_b)[None]


def solution(mesh):
    placed = (
        P("shot", None, "slab", None),
        P("shot", None, "slab", None),
        P("shot", None, "slab", None),
        P("shot", None),
        P("shot", None),
        P("shot", None, None),
        P("shot"),
        P("shot", None),
        P("shot", None, None),
    )
    return jax.shard_map(steps, mesh=mesh, in_specs=placed, out_specs=P("shot", None, "slab", None), check_vma=False)
```

```python
import functools

import jax
import jax.numpy as jnp
import numpy as np
from jax import lax
from jax.experimental import pallas as pl
from jax.experimental.pallas import tpu as pltpu
from jax.sharding import PartitionSpec as P


TILES_Y = 4
SCALE = 5040.0
STENCIL = (8064.0, -1008.0, 128.0, -9.0)
CENTRE_XZ = -43008.0
CENTRE_Y = -42.0

BX = 8
Z = 16
Y = 256
Y_BITS = 8
AX = 64
ROWS = BX * Z
BLOCKS = AX // BX
HALF = 128
HOT = 512
FLAT = AX * Z
F32 = jnp.float32
BF16 = jnp.bfloat16
VMEM = pl.BlockSpec(memory_space=pltpu.VMEM)
SMEM = pl.BlockSpec(memory_space=pltpu.SMEM)
HBM = pl.BlockSpec(memory_space=pltpu.HBM)
PIECES = 4


def weight(distance):
    distance = np.abs(distance)
    table = np.array((0.0,) + STENCIL + (0.0,))
    return table[np.minimum(distance, 5)]


def exact(matrix):
    narrow = matrix.astype(np.float32).astype(jnp.bfloat16)
    assert np.array_equal(narrow.astype(np.float64), matrix)
    return jnp.asarray(narrow)


def along_xz():
    out_x, out_z = np.divmod(np.arange(ROWS), Z)
    in_x, in_z = np.divmod(np.arange(2 * ROWS), Z)
    kinds = []
    for lead in (0, 4, 8):
        dx = out_x[:, None] - (in_x[None, :] - lead)
        dz = out_z[:, None] - in_z[None, :]
        both = np.where(dz == 0, weight(dx), 0.0) + np.where(dx == 0, weight(dz), 0.0)
        kinds.append(both + np.where((dx == 0) & (dz == 0), CENTRE_XZ, 0.0))
    return np.stack(kinds)


def along_y():
    at = np.arange(Y)
    return weight(at[:, None] - at[None, :]) + CENTRE_Y * np.eye(Y)


def dot(a, b):
    return jnp.dot(a, b, preferred_element_type=F32)


def split3(value):
    high = value.astype(BF16)
    rest = value - high.astype(F32)
    middle = rest.astype(BF16)
    return high, middle, (rest - middle.astype(F32)).astype(BF16)


def cost(flops, nbytes):
    return pl.CostEstimate(flops=flops, transcendentals=0, bytes_accessed=nbytes)


def rims(fwd, adj):
    front = lax.broadcasted_iota(jnp.int32, (BX, 8, Y), 1) < 4
    top = jnp.where(front, pltpu.roll(fwd[:, 8:, :], 4, 1), adj[:, 8:, :])
    bottom = jnp.where(front, fwd[:, :8, :], pltpu.roll(adj[:, :8, :], 4, 1))
    return top, bottom


def load_kernel(anchor_hbm, vel_hbm, fwd_hbm, adj_hbm, tagged, fwd, adj, up, down, flags, anchor, sems):
    anchor_copy = pltpu.make_async_copy(anchor_hbm, anchor, sems.at[2 * PIECES + 1])
    anchor_copy.start()
    rows = vel_hbm.shape[0]
    tile_copy = pltpu.make_async_copy(vel_hbm, tagged.at[pl.ds(0, rows)], sems.at[2 * PIECES])
    size = AX // PIECES
    copies = []
    for n, (source, target) in enumerate(((fwd_hbm, fwd), (adj_hbm, adj))):
        for i in range(PIECES):
            at = pl.ds(i * size, size)
            copies.append(pltpu.make_async_copy(source.at[at], target.at[at], sems.at[n * PIECES + i]))
    for copy in copies:
        copy.start()
    tile_copy.start()
    anchor_copy.wait()
    device = lax.axis_index("shot")
    home_row = device // TILES_Y
    home_col = device - home_row * TILES_Y
    part_row = home_row - anchor[0, 0]
    part_col = home_col - anchor[0, 1]
    side_row = 1 - 2 * part_row
    side_col = 1 - 2 * part_col
    toward_e = 1 - 2 * (home_row & 1)
    toward_a = 1 - 2 * (home_col & 1)
    flags[0] = part_row
    flags[1] = part_col
    flags[2] = jnp.where(side_row == toward_e, 1, 0)
    flags[3] = jnp.where(side_col == toward_a, 1, 0)
    flags[4] = toward_e
    flags[5] = toward_a
    tagged[rows] = jnp.full(tagged.shape[1:], side_row.astype(F32))
    tagged[rows + 1] = jnp.full(tagged.shape[1:], side_col.astype(F32))

    for copy in copies:
        copy.wait()

    def step(b, _):
        at = pl.ds(b * BX, BX)
        up[at], down[at] = rims(fwd[at], adj[at])
        return 0

    lax.fori_loop(0, BLOCKS, step, 0)
    tile_copy.wait()


def inner_laplace(b, parts, xz, y, result):
    pair = pl.ds(pl.multiple_of(b * 2 * ROWS, 2 * ROWS), 2 * ROWS)
    high, middle, low = parts
    total = dot(low[pair], y[...]) + dot(middle[pair], y[...]) + dot(high[pair], y[...])
    for i in range(2):
        block = 2 * b + i
        kind = jnp.where(block == 0, 0, jnp.where(block == BLOCKS - 1, 2, 1))
        first = jnp.clip(block * BX - 4, 0, AX - 2 * BX) * Z
        window = pl.ds(pl.multiple_of(first, 64), 2 * ROWS)
        part = dot(xz[kind], low[window]) + dot(xz[kind], middle[window]) + dot(xz[kind], high[window])
        result[pl.ds(pl.multiple_of(block * ROWS, ROWS), ROWS)] = part + total[i * ROWS : (i + 1) * ROWS]


def split_all(field, parts):
    def step(b, _):
        at = pl.ds(pl.multiple_of(b * ROWS, ROWS), ROWS)
        parts[0][at], parts[1][at], parts[2][at] = split3(field[at])
        return 0

    lax.fori_loop(0, BLOCKS, step, 0)


def table_of(cells, amounts, first_layer, total_depth, table):
    count = cells.shape[1]
    column = cells >> Y_BITS
    cell_x = ((column.astype(F32) + 0.5) * (1.0 / total_depth)).astype(jnp.int32)
    cell_z = column - cell_x * total_depth - first_layer
    inside = (cell_z >= 0) & (cell_z < Z)
    table[...] = jnp.full(table.shape, -1.0, F32)
    table[0:1, 0:count] = jnp.where(inside, cell_x * Z + cell_z, -1).astype(F32)
    table[1:2, 0:count] = (cells & (Y - 1)).astype(F32)
    table[2:3, 0:count] = amounts[0]
    table[3:4, 0:count] = amounts[1]


def ones_of(points, ones):
    def step(i, _):
        at = pl.ds(pl.multiple_of(i * 128, 128), 128)
        place = jnp.broadcast_to(points[1:2, at], (128, 128)).T
        y = lax.broadcasted_iota(jnp.int32, (128, 128), 1).astype(F32)
        for n in range(Y // 128):
            ones[at, pl.ds(n * 128, 128)] = jnp.where(place == y + float(n * 128), 1.0, 0.0).astype(BF16)
        return 0

    lax.fori_loop(0, points.shape[1] // 128, step, 0)


def hot_rows(b, points, n, hot):
    count = points.shape[1]
    amount = points[2 + n : 3 + n, :]
    part = amount.astype(BF16).astype(F32)
    rest = (amount - part).astype(BF16).astype(F32)
    rows = points[0:1, :].astype(jnp.int32)
    for i in range(HOT // 128):
        hit = lax.broadcasted_iota(jnp.int32, (128, count), 0) + (b * HOT + i * 128) == rows
        hot[pl.ds(i * 128, 128)] = jnp.where(hit, part, 0.0).astype(BF16)
        hot[pl.ds(HOT + i * 128, 128)] = jnp.where(hit, rest, 0.0).astype(BF16)


def inject_all(n, shots, receivers, shot_ones, receiver_ones, fwd_in, adj_in, shot_hot, hot):
    def step(b, _):
        at = pl.ds(pl.multiple_of(b * HOT, HOT), HOT)
        for points, ones, rows, field in ((shots, shot_ones, shot_hot, fwd_in), (receivers, receiver_ones, hot, adj_in)):
            hot_rows(b, points, n, rows)
            both = dot(rows[...], ones[...])
            field[at] = both[:HOT] + both[HOT:]
        return 0

    lax.fori_loop(0, FLAT // HOT, step, 0)


def inject_kernel(total_depth, shot_count, source_cell, wavelet, receiver_cell, residual,
                  fwd_in, adj_in, shots, receivers, shot_ones, receiver_ones, *hot):
    first_layer = lax.axis_index("slab") * Z
    active = lax.broadcasted_iota(jnp.int32, source_cell.shape, 1) < shot_count[0]
    waves = [jnp.where(active, wavelet[i : i + 1, :], 0.0) for i in range(2)]
    table_of(source_cell[...], waves, first_layer, total_depth, shots)
    table_of(receiver_cell[...], [residual[1:2, :], residual[0:1, :]], first_layer, total_depth, receivers)
    ones_of(shots, shot_ones)
    ones_of(receivers, receiver_ones)
    inject_all(0, shots, receivers, shot_ones, receiver_ones, fwd_in, adj_in, *hot)


def inject_again_kernel(shots, receivers, shot_ones, receiver_ones, fwd_in, adj_in, *hot):
    inject_all(1, shots, receivers, shot_ones, receiver_ones, fwd_in, adj_in, *hot)


def laplace_kernel(fwd, adj, xz, y, lap_fwd, lap_adj, f0, f1, f2, a0, a1, a2):
    split_all(fwd, (f0, f1, f2))
    split_all(adj, (a0, a1, a2))

    def step(b, _):
        inner_laplace(b, (f0, f1, f2), xz, y, lap_fwd)
        inner_laplace(b, (a0, a1, a2), xz, y, lap_adj)
        return 0

    lax.fori_loop(0, BLOCKS // 2, step, 0)


def halo_weights():
    row = lax.broadcasted_iota(jnp.int32, (8, HALF), 0)
    low = [jnp.where(row + k <= 3, STENCIL[3 - k], 0.0) for k in range(4)]
    high = [jnp.where(row - 4 - k >= 0, STENCIL[3 - k], 0.0) for k in range(4)]
    return low, high


def halo_of(x, lanes, below, above, weights):
    at = pl.ds(pl.multiple_of(x * 8, 8), 8)
    low, high = weights
    under = below[at, lanes]
    over = above[at, lanes]
    fields = []
    for field in (0, 1):
        parts = []
        for rows, weight_of, shifts in (
            (under, low, [(8 - 4 * field - k) % 8 for k in range(4)]),
            (over, high, [(4 - 4 * field + k) % 8 for k in range(4)]),
        ):
            terms = [w * (pltpu.roll(rows, n, 0) if n else rows) for w, n in zip(weight_of, shifts)]
            parts.append((terms[0] + terms[1]) + (terms[2] + terms[3]))
        fields.append(jnp.concatenate(parts, 0))
    return fields


def advance_kernel(flags, own, col_a, col_b, row_e, row_o, diag_e, diag_o, lap_fwd, lap_adj, fwd, adj, fwd_in, adj_in,
                   below, above, speed2, mid_fwd, mid_adj, up, down):
    half = col_b.shape[0]
    wide = own.shape[2]
    with_e = flags[2] == 1
    with_a = flags[3] == 1
    row_at = flags[0] * half
    row_to = (1 - flags[0]) * half
    col_at = pl.ds(pl.multiple_of(flags[1] * wide, wide), wide)
    col_to = pl.ds(pl.multiple_of((1 - flags[1]) * wide, wide), wide)

    def assemble(i, _):
        at = pl.ds(i * 8, 8)
        near = pl.ds(row_at + i * 8, 8)
        far = pl.ds(row_to + i * 8, 8)
        speed = own[at]
        speed2[near, :, col_at] = speed * speed * (1.0 / SCALE)
        speed = jnp.where(with_a, col_a[at], col_b[at])
        speed2[near, :, col_to] = speed * speed * (1.0 / SCALE)
        speed = jnp.where(with_e, row_e[at], row_o[at])
        speed2[far, :, col_at] = speed * speed * (1.0 / SCALE)
        speed = jnp.where(with_e, diag_e[at], diag_o[at])
        speed2[far, :, col_to] = speed * speed * (1.0 / SCALE)
        return 0

    lax.fori_loop(0, half // 8, assemble, 0)

    weights = halo_weights()
    front = lax.broadcasted_iota(jnp.int32, (8, HALF), 0) < 4

    def step(x, _):
        at = pl.ds(pl.multiple_of(x * Z, Z), Z)
        for h in range(Y // HALF):
            lanes = pl.ds(h * HALF, HALF)
            halo_fwd, halo_adj = halo_of(x, lanes, below, above, weights)
            c = speed2[x, :, lanes]
            new_fwd = fwd[at, lanes] + (c * (lap_fwd[at, lanes] + halo_fwd) + fwd_in[at, lanes])
            new_adj = adj[at, lanes] + (c * (lap_adj[at, lanes] + halo_adj) + adj_in[at, lanes])
            mid_fwd[at, lanes] = new_fwd
            mid_adj[at, lanes] = new_adj
            up[x, :, lanes] = jnp.where(front, pltpu.roll(new_fwd[8:], 4, 0), new_adj[8:])
            down[x, :, lanes] = jnp.where(front, new_fwd[:8], pltpu.roll(new_adj[:8], 4, 0))
        return 0

    lax.fori_loop(0, AX, step, 0, unroll=2)


def blend_kernel(speed2, lap_fwd, lap_adj, fwd, adj, mid_fwd, mid_adj, fwd_in, adj_in, inner, by_adj, by_fwd):
    def step(b, _):
        at = pl.ds(pl.multiple_of(b * Z * 2, Z * 2), Z * 2)
        c = speed2[at]
        later = mid_adj[at]
        first = mid_fwd[at] - fwd[at]
        second_fwd = c * lap_fwd[at] + fwd_in[at]
        earlier = 2.0 * later - adj[at] + (c * lap_adj[at] + adj_in[at])
        inner[at] = earlier * first + later * second_fwd
        by_adj[at] = c * first
        by_fwd[at] = c * later
        return 0

    lax.fori_loop(0, FLAT // (Z * 2), step, 0, unroll=2)


def image_kernel(flags, inner, by_adj, by_fwd, below, above, own, col, row, diag, image):
    weights = halo_weights()

    def step(x, _):
        at = pl.ds(pl.multiple_of(x * Z, Z), Z)
        for h in range(Y // HALF):
            lanes = pl.ds(h * HALF, HALF)
            halo_fwd, halo_adj = halo_of(x, lanes, below, above, weights)
            image[x, :, lanes] = inner[at, lanes] + by_adj[at, lanes] * halo_adj + by_fwd[at, lanes] * halo_fwd
        return 0

    lax.fori_loop(0, AX, step, 0, unroll=2)
    half = own.shape[0]
    wide = own.shape[2]
    row_at = flags[0] * half
    row_to = (1 - flags[0]) * half
    col_at = pl.ds(pl.multiple_of(flags[1] * wide, wide), wide)
    col_to = pl.ds(pl.multiple_of((1 - flags[1]) * wide, wide), wide)

    def hand_out(i, _):
        at = pl.ds(i * 8, 8)
        near = pl.ds(row_at + i * 8, 8)
        far = pl.ds(row_to + i * 8, 8)
        own[at] = image[near, :, col_at]
        col[at] = image[near, :, col_to]
        row[at] = image[far, :, col_at]
        diag[at] = image[far, :, col_to]
        return 0

    lax.fori_loop(0, half // 8, hand_out, 0)


def swaps(count):
    rows = count // TILES_Y
    a = [(s, s ^ 1) for s in range(count)]
    b = [(s, s + 1) if s % TILES_Y == 1 else (s, s - 1) for s in range(count) if s % TILES_Y in (1, 2)]
    e = [(s, s + TILES_Y if (s // TILES_Y) % 2 == 0 else s - TILES_Y) for s in range(count)]
    o = []
    for s in range(count):
        other = s // TILES_Y + (1 if (s // TILES_Y) % 2 else -1)
        if 0 <= other < rows:
            o.append((s, other * TILES_Y + s % TILES_Y))
    return a, b, e, o


def select_kernel(flags, col_a, col_b, row_e, row_o, diag_e, diag_o, tag_e, tag_o):
    half = col_b.shape[0]
    toward_a = flags[5].astype(F32)
    tag_e[...] = row_e[half:]
    tag_o[...] = row_o[half:]
    e_wants_a = row_e[half + 1] == toward_a
    o_wants_a = row_o[half + 1] == toward_a

    def step(i, _):
        at = pl.ds(i * 8, 8)
        a = col_a[at]
        b = col_b[at]
        diag_e[at] = jnp.where(e_wants_a[None], a, b)
        diag_o[at] = jnp.where(o_wants_a[None], a, b)
        return 0

    lax.fori_loop(0, half // 8, step, 0)


def bucket_kernel(flags, col, back_e, back_o, tag_e, tag_o, sum_a, sum_b):
    toward_e = flags[4].astype(F32)
    toward_a = flags[5].astype(F32)
    with_a = flags[3] == 1
    from_e = tag_e[0] == -toward_e
    from_o = tag_o[0] == toward_e
    e_a = from_e & (tag_e[1] == toward_a)
    e_b = from_e & (tag_e[1] == -toward_a)
    o_a = from_o & (tag_o[1] == toward_a)
    o_b = from_o & (tag_o[1] == -toward_a)

    def step(i, _):
        at = pl.ds(i * 8, 8)
        c = col[at]
        e = back_e[at]
        o = back_o[at]
        sum_a[at] = jnp.where(with_a, c, 0.0) + jnp.where(e_a[None], e, 0.0) + jnp.where(o_a[None], o, 0.0)
        sum_b[at] = jnp.where(with_a, 0.0, c) + jnp.where(e_b[None], e, 0.0) + jnp.where(o_b[None], o, 0.0)
        return 0

    lax.fori_loop(0, col.shape[0] // 8, step, 0)


def near_kernel(flags, tile, own, same_e, same_o, tag_e, tag_o, sum_a, near, twice):
    toward_e = flags[4].astype(F32)
    from_e = tag_e[0] == -toward_e
    from_o = tag_o[0] == toward_e

    def step(i, _):
        at = pl.ds(i * 8, 8)
        total = own[at] + jnp.where(from_e[None], same_e[at], 0.0) + jnp.where(from_o[None], same_o[at], 0.0)
        double = 2.0 * tile[at]
        twice[at] = double
        near[at] = double * (total + sum_a[at])
        return 0

    lax.fori_loop(0, own.shape[0] // 8, step, 0)


def steps(velocity, fwd_field, adj_field, aperture_anchor, source_cell, wavelet, shot_count, receiver_cell, residual):
    tile = velocity[0]
    half, depth, wide = tile.shape
    slabs = lax.axis_size("slab")
    pair_a, pair_b, pair_e, pair_o = swaps(lax.axis_size("shot"))
    to_up = [(i, i + 1) for i in range(slabs - 1)]
    to_down = [(i + 1, i) for i in range(slabs - 1)]

    def shape(*dims, dtype=F32):
        return jax.ShapeDtypeStruct(dims, dtype)

    def send(pairs, value, axis="shot"):
        return lax.ppermute(value, axis, pairs)

    def kernel(function, ins, outs, args, flops, mib=8, scratch=()):
        places = [{"s": SMEM, "h": HBM, "v": VMEM}[i] for i in ins]
        sent = tuple(SMEM if o.dtype == jnp.int32 else VMEM for o in outs)
        nbytes = sum(int(np.prod(a.shape)) * 4 for a in tuple(args) + tuple(outs))
        return pl.pallas_call(
            function,
            out_shape=tuple(outs),
            in_specs=places,
            out_specs=sent,
            scratch_shapes=list(scratch),
            compiler_params=pltpu.CompilerParams(vmem_limit_bytes=mib * 1024 * 1024),
            cost_estimate=cost(flops, nbytes),
        )(*args)

    piece = shape(half, depth, wide)
    rim_shape = shape(AX, 8, Y)
    flat = shape(FLAT, Y)
    parts = [pltpu.VMEM((FLAT, Y), BF16)] * 6
    inner = (exact(along_xz()), exact(along_y()))

    col_b = send(pair_b, tile)
    field = shape(AX, depth, Y)
    tagged, fwd, adj, up, down, flags = kernel(
        load_kernel, "hhhh",
        (shape(half + 2, depth, wide), field, field, rim_shape, rim_shape, shape(8, dtype=jnp.int32)),
        tuple(pltpu.with_memory_space_constraint(v, pltpu.HBM) for v in (aperture_anchor, tile, fwd_field[0], adj_field[0])), 1 << 20, 8, [pltpu.SMEM((1, 2), jnp.int32), pltpu.SemaphoreType.DMA((2 * PIECES + 2,))])
    flat_fwd = fwd.reshape(FLAT, Y)
    flat_adj = adj.reshape(FLAT, Y)
    col_a = send(pair_a, tagged)
    row_e = send(pair_e, tagged)
    row_o = send(pair_o, tagged)
    below = send(to_up, up, "slab")
    above = send(to_down, down, "slab")
    recv = receiver_cell.shape[1]

    hot = [pltpu.VMEM((2 * HOT, n), BF16) for n in (128, recv)]
    ones = (shape(128, Y, dtype=BF16), shape(recv, Y, dtype=BF16))
    fwd_in1, adj_in1, *points = kernel(
        functools.partial(inject_kernel, depth * slabs), "svvvv",
        (flat, flat, shape(8, 128), shape(8, recv)) + ones,
        (shot_count, source_cell, wavelet[0], receiver_cell, residual[0]), 2 << 30, 12, hot)
    diag_e, diag_o, tag_e, tag_o = kernel(
        select_kernel, "svvvv", (piece, piece, shape(2, depth, wide), shape(2, depth, wide)),
        (flags, col_a, col_b, row_e, row_o), 1 << 20)
    diag_e = send(pair_e, diag_e)
    diag_o = send(pair_o, diag_o)
    lap_fwd, lap_adj = kernel(
        laplace_kernel, "vvvv", (flat,) * 2, (flat_fwd, flat_adj) + inner, 2 << 30, 8, parts)
    speed2, mid_fwd, mid_adj, up, down = kernel(
        advance_kernel, "s" + "v" * 15, (shape(AX, depth, Y), flat, flat, rim_shape, rim_shape),
        (flags, tagged, col_a, col_b, row_e, row_o, diag_e, diag_o, lap_fwd, lap_adj, flat_fwd, flat_adj, fwd_in1, adj_in1,
         below.reshape(AX * 8, Y), above.reshape(AX * 8, Y)), 4 << 20)
    below = send(to_up, up, "slab")
    above = send(to_down, down, "slab")
    lap_fwd, lap_adj = kernel(laplace_kernel, "vvvv", (flat,) * 2, (mid_fwd, mid_adj) + inner, 2 << 30, 8, parts)
    fwd_in2, adj_in2 = kernel(inject_again_kernel, "vvvv", (flat, flat), tuple(points), 2 << 30, 12, hot)
    inner_part, by_adj, by_fwd = kernel(
        blend_kernel, "v" * 9, (flat,) * 3,
        (speed2.reshape(FLAT, Y), lap_fwd, lap_adj, flat_fwd, flat_adj, mid_fwd, mid_adj, fwd_in2, adj_in2), 4 << 20)
    own, col, row, diag = kernel(
        image_kernel, "s" + "v" * 5, (piece,) * 4,
        (flags, inner_part, by_adj, by_fwd, below.reshape(AX * 8, Y), above.reshape(AX * 8, Y)),
        4 << 20, 8, [pltpu.VMEM((AX, depth, Y), F32)])
    back_e = send(pair_e, diag)
    back_o = send(pair_o, diag)
    sum_a, sum_b = kernel(
        bucket_kernel, "svvvvv", (piece,) * 2, (flags, col, back_e, back_o, tag_e, tag_o), 1 << 20)
    sum_b = send(pair_b, sum_b)
    sum_a = send(pair_a, sum_a)
    same_e = send(pair_e, row)
    same_o = send(pair_o, row)
    near, twice = kernel(
        near_kernel, "s" + "v" * 7, (piece, piece), (flags, tagged, own, same_e, same_o, tag_e, tag_o, sum_a), 1 << 20)
    return (near + twice * sum_b)[None]


def solution(mesh):
    placed = (
        P("shot", None, "slab", None),
        P("shot", None, "slab", None),
        P("shot", None, "slab", None),
        P("shot", None),
        P("shot", None),
        P("shot", None, None),
        P("shot"),
        P("shot", None),
        P("shot", None, None),
    )
    return jax.shard_map(steps, mesh=mesh, in_specs=placed, out_specs=P("shot", None, "slab", None), check_vma=False)
```
